1024 devices in a mesh: row: 128 (over x, z, core), col: 8 (over y).
Axes of the slice: x: 8, y: 8, z: 8, core: 2. Of those that a mesh axis runs over, the one named last changes fastest.
Arguments:
- p2_panel: bfloat16 [65536, 3584], P('row'), may hold values from -6 to 6
- density: bfloat16 [65536, 3584], P('row', 'col'), may hold values from -0.09375 to 0.09375
- pattern: int32 [1024, 56], P('row'), may hold values 0 or 1
- x_basis: bfloat16 [65536, 32], P('row'), may hold values from -0.59765625 to 0.59765625
- x_offset: int32 [1024], P('row'), may hold values from 0 to 160
- x_extent: int32 [1024], P('row'), may hold values from 1 to 32
- y_basis: bfloat16 [128, 3584, 32], P('row', 'col'), may hold values from -0.59765625 to 0.59765625
- y_offset: int32 [128, 56], P('row', 'col'), may hold values from 0 to 160
- y_extent: int32 [128, 56], P('row', 'col'), may hold values from 1 to 32
Outputs:
- new_density: bfloat16 [65536, 3584], P('row', 'col')
- grid_density: float32 [16384, 1024], P('row', 'col')
The draws below stay inside these ranges and needn't reach their ends.
Inputs may be any that keep to these rules, and one draw needn't show every extreme that they name: `pattern`: 1 where a block of the window is stored.
All inputs are finite; a program needn't handle non-finite values.
Results may differ from the reference program's by a relative error of at most 0.0049.
Values may be sent and summed in bfloat16 or wider, within the bound.
A program may use at most 64 MiB of HBM per device.

```python
import jax
import jax.numpy as jnp
from jax import lax

BS = 64
BR = 8
HD = 3
SX = 128
SY = 128
TX = 32
TY = 32
M = 32
NB = 1024
W = 56
WC = 7
NX = 16384
NY = 1024
N_ROW = 128
N_COL = 8


def touch_ends(array, own_key, low, largest):
    spot = [jax.random.randint(jax.random.fold_in(own_key, axis), (), 0, length) for axis, length in enumerate(array.shape)]
    widest = array.shape.index(max(array.shape))
    beside = spot[:widest] + [(spot[widest] + 1) % array.shape[widest]] + spot[widest + 1:]
    return array.at[tuple(spot)].set(low).at[tuple(beside)].set(largest)


def block_scale(key, dims, cuts, smallest, top_value):
    level, own = 1.0, jax.random.fold_in(key, 6)
    for dim, parts in cuts:
        draws = jnp.exp(jax.random.uniform(jax.random.fold_in(own, dim), (parts,), jnp.float32, smallest / len(cuts), top_value / len(cuts)))
        level = level * jnp.repeat(draws, dims[dim] // parts).reshape([-1 if axis == dim else 1 for axis in range(len(dims))])
    return level


def normal_values(own_key, shape, scale, bound, shards=(), held_as=jnp.bfloat16):
    gain = block_scale(own_key, shape, shards, -0.22, 0.18) if shards else 1.0
    values = jax.random.normal(own_key, shape, jnp.float32) * scale * gain
    return jnp.minimum(jnp.maximum(values, -bound), bound).astype(held_as)


def setup_inputs(seed: int = 0) -> dict:
    splits = jax.random.split(jax.random.key(seed), 10)
    return {
        "p2_panel": normal_values(splits[0], (NB * BS, W * BS), 1.0, 6.0, ((0, 128),)),
        "density": normal_values(splits[1], (NB * BS, W * BS), (W * BS) ** -0.5, 0.09375, ((0, 128), (1, 8))),
        "pattern": touch_ends((jax.random.randint(splits[2], (NB, W), 0, 4) < 3).astype(jnp.int32), jax.random.fold_in(splits[2], 1), 0, 1),
        "x_basis": normal_values(splits[3], (NB * BS, TX), 0.1, 0.59765625, ((0, 128),)),
        "x_offset": touch_ends(jax.random.randint(splits[4], (NB,), 0, SX + 2 * M - TX + 1), jax.random.fold_in(splits[4], 1), 0, SX + 2 * M - TX).astype(jnp.int32),
        "x_extent": touch_ends(jax.random.randint(splits[5], (NB,), 1, TX + 1), jax.random.fold_in(splits[5], 1), 1, TX).astype(jnp.int32),
        "y_basis": normal_values(splits[6], (N_ROW, W * BS, TY), 0.1, 0.59765625, ((0, 128), (1, 8))),
        "y_offset": touch_ends(jax.random.randint(splits[7], (N_ROW, W), 0, SY + 2 * M - TY + 1), jax.random.fold_in(splits[7], 1), 0, SY + 2 * M - TY).astype(jnp.int32),
        "y_extent": touch_ends(jax.random.randint(splits[8], (N_ROW, W), 1, TY + 1), jax.random.fold_in(splits[8], 1), 1, TY).astype(jnp.int32),
    }


def mask_blocks(values, pattern):
    number, win_slots = pattern.shape
    block_size = values.shape[0] // number
    shaped = values.reshape(number, block_size, win_slots, block_size)
    return (shaped * pattern.astype(values.dtype)[:, None, :, None]).reshape(values.shape)


def place(tile_vals, offset, extent, length):
    number = offset.shape[0]
    breadth = tile_vals.shape[1]
    blocks = tile_vals.reshape(number, -1, breadth).astype(jnp.float32)
    cell_ids = jnp.arange(length, dtype=jnp.int32)
    step_ids = jnp.arange(breadth, dtype=jnp.int32)
    onehot = (cell_ids[None, None, :] == offset[:, None, None] + step_ids[None, :, None]) & (step_ids[None, :, None] < extent[:, None, None])
    spread = jnp.einsum("iat,ite->iae", blocks, onehot.astype(jnp.float32))
    return spread.reshape(-1, length).astype(jnp.bfloat16)


def natural_order(values):
    height = values.shape[0]
    return values.reshape(height, N_COL, WC, BS).transpose(0, 2, 1, 3).reshape(height, W * BS)


def class_order(values):
    height = values.shape[0]
    return values.reshape(height, WC, N_COL, BS).transpose(0, 2, 1, 3).reshape(height, W * BS)


def pick(values, index):
    return lax.dynamic_index_in_dim(values, index, 0, keepdims=False)


def reference(p2_panel, density, pattern, x_basis, x_offset, x_extent, y_basis, y_offset, y_extent):
    panel_rows = BR * BS
    square = mask_blocks(p2_panel, pattern).reshape(N_ROW, panel_rows, W * BS)
    stored = mask_blocks(natural_order(density), pattern).reshape(N_ROW, panel_rows, W * BS)
    patterns = pattern.reshape(N_ROW, BR, W)
    x_values = x_basis.reshape(N_ROW, panel_rows, TX)
    x_starts = x_offset.reshape(N_ROW, BR)
    x_sizes = x_extent.reshape(N_ROW, BR)

    def one_panel(panel):
        pieces = []
        for distance in range(-HD, HD + 1):
            source = pick(stored, (panel + distance) % N_ROW)
            cut_cols = BR * abs(distance) * BS
            if distance > 0:
                aligned = jnp.concatenate([jnp.zeros((panel_rows, cut_cols), source.dtype), source[:, : W * BS - cut_cols]], axis=1)
            elif distance < 0:
                aligned = jnp.concatenate([source[:, cut_cols:], jnp.zeros((panel_rows, cut_cols), source.dtype)], axis=1)
            else:
                aligned = source
            pieces.append(aligned)
        window = jnp.concatenate(pieces, axis=0)
        own_rows = pick(square, panel)
        product = jnp.dot(own_rows, window, preferred_element_type=jnp.float32)
        own_pattern = pick(patterns, panel)
        renewed = mask_blocks(3.0 * own_rows.astype(jnp.float32) - 2.0 * product, own_pattern).astype(jnp.bfloat16)
        renewed = class_order(renewed)
        y_spread = place(pick(y_basis, panel), pick(y_offset, panel), pick(y_extent, panel), SY + 2 * M)
        left_side = renewed.reshape(panel_rows, N_COL, WC * BS).astype(jnp.float32)
        right_side = y_spread.reshape(N_COL, WC * BS, SY + 2 * M).astype(jnp.float32)
        half_done = jnp.einsum("xcj,cjy->cxy", left_side, right_side).astype(jnp.bfloat16)
        x_spread = place(pick(x_values, panel), pick(x_starts, panel), pick(x_sizes, panel), SX + 2 * M)
        extended = jnp.einsum("xe,cxf->cef", x_spread.astype(jnp.float32), half_done.astype(jnp.float32))
        return renewed, extended

    renewed_all, extended = lax.map(one_panel, jnp.arange(N_ROW, dtype=jnp.int32))
    interior = extended[:, :, M:M + SX, :]
    interior = interior.at[:, :, SX - M:, :].add(jnp.roll(extended[:, :, :M, :], -1, axis=0))
    interior = interior.at[:, :, :M, :].add(jnp.roll(extended[:, :, SX + M:, :], 1, axis=0))
    grid_out = interior[:, :, :, M:M + SY]
    grid_out = grid_out.at[:, :, :, SY - M:].add(jnp.roll(interior[:, :, :, :M], -1, axis=1))
    grid_out = grid_out.at[:, :, :, :M].add(jnp.roll(interior[:, :, :, SY + M:], 1, axis=1))
    grid_density = grid_out.transpose(0, 2, 1, 3).reshape(NX, NY)
    return renewed_all.reshape(NB * BS, W * BS), grid_density
```

```python
import functools

import jax
import jax.numpy as jnp
from jax import lax
from jax.experimental import pallas as pl
from jax.experimental.pallas import tpu as pltpu
from jax.sharding import PartitionSpec as P

MESH = pl.DeviceIdType.MESH
BS = 64
BR = 8
CLASSES = 8
WC = 7
W = 56
PANEL = 512
TILE = 128
CELLS = 192
SX = 128
MARGIN = 32
F32 = jnp.float32
BF16 = jnp.bfloat16

UP = {
    1: ((320, 128), (192, 128), (64, 128)),
    2: ((320, 128), (192, 128), (128, 64)),
    3: ((320, 128), (192, 128)),
}
DOWN = {
    1: ((0, 128), (128, 128), (256, 128)),
    2: ((0, 128), (128, 128), (256, 64)),
    3: ((0, 128), (128, 128)),
}
FIRST = {1: 0, 2: 3, 3: 6}
BASE = {1: 0, 2: 384, 3: 704}
IN_ROWS = 960


def dot_nt(left, right):
    return lax.dot_general(left, right, (((1,), (1,)), ((), ())), preferred_element_type=F32)


def kernel(
    rows, cols,
    p2, dens, pat, xb, xo, xe, yb, yo, ye,
    out_new, out_grid,
    s, dv, pv, xbv, ybv, xov, xev, yov, yev,
    own, up_in, down_in, acc, spread_x, spread_y, mask_rows, ext, packed, halo,
    load_sem, send_sem, up_sem, down_sem, hsend_sem, halo_sem,
):
    r = lax.axis_index("row")
    c = lax.axis_index("col")
    even = lax.rem(r, 2) == 0
    odd = lax.rem(r, 2) == 1

    def at(dr, dc):
        return (lax.rem(r + (dr + rows), rows), lax.rem(c + (dc + cols), cols))

    barrier = pltpu.get_barrier_semaphore()
    friends = [(-1, 0), (1, 0), (-2, 0), (2, 0), (0, -1), (0, 1), (-1, -1), (-1, 1), (1, -1), (1, 1)]
    for dr, dc in friends:
        pl.semaphore_signal(barrier, inc=1, device_id=at(dr, dc), device_id_type=MESH)

    loads = []
    for number, (source, target) in enumerate(
        ((dens, dv), (pat, pv), (xb, xbv), (yb, ybv), (xo, xov), (xe, xev), (yo, yov), (ye, yev))
    ):
        loads.append(pltpu.make_async_copy(source, target, load_sem.at[number]))
    square_loads = {}
    for number, block in enumerate((3, 2, 4, 1, 5, 0, 6)):
        part = pl.ds(block * PANEL, PANEL)
        square_loads[block] = pltpu.make_async_copy(p2.at[:, part], s.at[:, part], load_sem.at[8 + number])
    for load in loads:
        load.start()
    for block in (3, 2, 4, 1, 5, 0, 6):
        square_loads[block].start()

    loads[1].wait()
    pattern = pv[...].astype(F32).astype(BF16)
    position = lax.broadcasted_iota(jnp.int32, (BR, W), 1)
    slot = lax.broadcasted_iota(jnp.int32, (BR, W), 0)
    chosen = jnp.where(position == slot * CLASSES + c, 1.0, 0.0).astype(BF16)
    by_slot = dot_nt(chosen, pattern)
    block_row = lax.broadcasted_iota(jnp.int32, (BR, PANEL), 0)
    row_block = lax.broadcasted_iota(jnp.int32, (BR, PANEL), 1) // BS
    widen = jnp.where(block_row == row_block, 1.0, 0.0).astype(BF16)
    mask_rows[...] = jnp.dot(by_slot.astype(BF16), widen, preferred_element_type=F32)

    loads[0].wait()
    for k in range(WC):
        part = pl.ds(k * BS, BS)
        keep = jnp.broadcast_to(mask_rows[k : k + 1, :], (BS, PANEL)).astype(BF16)
        own[part, :] = dv[part, :] * keep

    pl.semaphore_wait(barrier, len(friends))

    def send(source, landing, sem, number, place):
        return pltpu.make_async_remote_copy(
            src_ref=source,
            dst_ref=landing,
            send_sem=send_sem.at[number],
            recv_sem=sem,
            device_id=place,
            device_id_type=MESH,
        )

    sides = {
        "even": (UP, up_in, up_sem, 1),
        "odd": (DOWN, down_in, down_sem, -1),
    }

    def landing(kind, d, chunk):
        first, count = chunk
        start = BASE[d] + first - (d * BS if kind == "even" else 0)
        return sides[kind][1].at[pl.ds(start, count)]

    def sends(kind):
        chunks, _, sem, sign = sides[kind]
        other = "odd" if kind == "even" else "even"
        other_chunks, _, other_sem, _ = sides[other]
        found = []
        for j in range(3):
            one, two = FIRST[1] + j, FIRST[2] + j
            far, near, back = chunks[2][j], chunks[1][j], other_chunks[1][j]
            found.append(send(own.at[pl.ds(*far)], landing(kind, 2, far), sem.at[two], 3 + j, at(2 * sign, 0)))
            found.append(send(own.at[pl.ds(*back)], landing(other, 1, back), other_sem.at[one], 6 + j, at(-sign, 0)))
            found.append(send(own.at[pl.ds(*near)], landing(kind, 1, near), sem.at[one], j, at(sign, 0)))
        return found

    @pl.when(even)
    def _():
        for copy in sends("even"):
            copy.start()

    @pl.when(odd)
    def _():
        for copy in sends("odd"):
            copy.start()

    def relays(kind, d, j):
        chunks, _, sem, sign = sides[kind]
        found = []

        def relay(to, number, place):
            chunk = chunks[to][j]
            found.append(
                send(landing(kind, d, chunk), landing(kind, to, chunk), sem.at[FIRST[to] + j], number, place)
            )

        if d == 1:
            if j < 2:
                relay(3, 9 + j, at(2 * sign, 0))
            relay(2, 11 + j, at(sign, 0))
        if d == 2 and j < 2:
            relay(3, 14 + j, at(sign, 0))
        return found

    def arrived(kind, d, j):
        chunks, _, sem, _ = sides[kind]
        place = landing(kind, d, chunks[d][j])
        send(place, place, sem.at[FIRST[d] + j], 0, at(-1, 0)).wait_recv()
        if d < 3:
            @pl.when(even if kind == "even" else odd)
            def _():
                for copy in relays(kind, d, j):
                    copy.start()

    position = lax.broadcasted_iota(jnp.int32, (W, PANEL), 0)
    natural = lax.broadcasted_iota(jnp.int32, (W, PANEL), 1) // BS
    for block in (3, 2, 4, 1, 5, 0, 6):
        square_loads[block].wait()
        chosen = jnp.where(position == natural + block * BR, 1.0, 0.0).astype(BF16)
        mask = jnp.dot(pattern, chosen, preferred_element_type=F32)
        for i in range(BR):
            keep = jnp.broadcast_to(mask[i : i + 1, :], (BS, PANEL)).astype(BF16)
            part = pl.ds(i * BS, BS)
            s[part, pl.ds(block * PANEL, PANEL)] = s[part, pl.ds(block * PANEL, PANEL)] * keep

    parity = lax.rem(c, 2)
    to_row = lax.broadcasted_iota(jnp.int32, (BS, TILE), 0)
    from_lane = lax.broadcasted_iota(jnp.int32, (BS, TILE), 1)
    pick = jnp.where(from_lane == to_row + parity * BS, -1.5, 0.0).astype(BF16)
    acc[...] = dot_nt(own[...], s[:, pl.ds(3 * PANEL, PANEL)])
    for k in range(WC):
        start = pl.multiple_of(k * PANEL + (c // 2) * TILE, TILE)
        part = pl.ds(k * BS, BS)
        acc[part, :] = acc[part, :] + dot_nt(pick, s[:, pl.ds(start, TILE)])

    def gather(kind, d, j):
        first, count = sides[kind][0][d][j]
        block = 3 - d if kind == "even" else 3 + d
        part = pl.ds(first - d * BS if kind == "even" else first + d * BS, count)
        place = landing(kind, d, (first, count))
        acc[part, :] = acc[part, :] + dot_nt(place[...], s[:, pl.ds(block * PANEL, PANEL)])

    for load in loads[2:]:
        load.wait()
    step_ids = lax.broadcasted_iota(jnp.int32, (2 * TILE, 32), 1)
    row_ids = lax.broadcasted_iota(jnp.int32, (2 * TILE, 32), 0)
    cell_ids = jnp.where(
        row_ids < CELLS - MARGIN, row_ids + MARGIN, jnp.where(row_ids < CELLS, row_ids - (CELLS - MARGIN), -1)
    )
    low = lax.broadcasted_iota(jnp.int32, (2 * TILE, TILE), 1) < BS

    def spread(values, offset, extent):
        hit = (cell_ids == offset + step_ids) & (step_ids < extent)
        onehot = jnp.where(hit, 1.0, 0.0).astype(BF16)
        return jnp.dot(onehot, values, preferred_element_type=F32)

    for t in range(4):
        part = pl.ds(t * TILE, TILE)
        pair = [spread(xbv[:, part], xov[2 * t + h], xev[2 * t + h]) for h in range(2)]
        spread_x[:, part] = jnp.where(low, pair[0], pair[1])[:CELLS].astype(BF16)
        if t < 3:
            pair = [spread(ybv[:, part], yov[0, 2 * t + h], yev[0, 2 * t + h]) for h in range(2)]
            spread_y[:, part] = jnp.where(low, pair[0], pair[1]).astype(BF16)
        else:
            part = pl.ds(t * TILE, BS)
            spread_y[:, part] = spread(ybv[:, part], yov[0, 6], yev[0, 6]).astype(BF16)

    for j in range(3):
        for d in (1, 2):
            for kind in ("even", "odd"):
                arrived(kind, d, j)
                gather(kind, d, j)
    for j in range(2):
        for kind in ("even", "odd"):
            arrived(kind, 3, j)
            gather(kind, 3, j)

    for k in range(WC):
        part = pl.ds(k * BS, BS)
        keep = jnp.broadcast_to(mask_rows[k : k + 1, :] * -2.0, (BS, PANEL))
        out_new[part, :] = (acc[part, :] * keep).astype(BF16)
    half_done = jnp.dot(spread_y[...], out_new[...], preferred_element_type=F32).astype(BF16)
    ext[...] = dot_nt(spread_x[...], half_done)

    def rim(number, source, place):
        return pltpu.make_async_remote_copy(
            src_ref=source,
            dst_ref=halo.at[number],
            send_sem=hsend_sem.at[number],
            recv_sem=halo_sem.at[number],
            device_id=place,
            device_id_type=MESH,
        )

    high_rows, low_rows = pl.ds(SX, MARGIN), pl.ds(SX + MARGIN, MARGIN)
    rims = [
        rim(4, ext.at[high_rows, pl.ds(TILE, TILE)], at(1, 1)),
        rim(5, ext.at[high_rows, pl.ds(TILE, TILE)], at(1, -1)),
        rim(6, ext.at[low_rows, pl.ds(TILE, TILE)], at(-1, 1)),
        rim(7, ext.at[low_rows, pl.ds(TILE, TILE)], at(-1, -1)),
        rim(0, ext.at[high_rows, pl.ds(0, TILE)], at(1, 0)),
        rim(1, ext.at[low_rows, pl.ds(0, TILE)], at(-1, 0)),
    ]
    for copy in rims:
        copy.start()
    lane = lax.broadcasted_iota(jnp.int32, (MARGIN, TILE), 1)
    group = lane // MARGIN
    margins = [jnp.zeros((MARGIN, TILE), F32), jnp.zeros((MARGIN, TILE), F32)]
    for g in range(4):
        piece = ext[g * MARGIN : (g + 1) * MARGIN, TILE : 2 * TILE]
        for side in range(2):
            turn = (MARGIN * (g - side)) % TILE
            turned = pltpu.roll(piece, turn, 1) if turn else piece
            margins[side] = jnp.where(group == g, turned, margins[side])
    packed[0] = margins[0]
    packed[1] = margins[1]
    late = [rim(2, packed.at[0], at(0, 1)), rim(3, packed.at[1], at(0, -1))]
    for copy in late:
        copy.start()

    for number in (0, 1, 2, 3, 4, 5, 6, 7):
        rim(number, halo.at[number], at(1, 0)).wait_recv()
    first, last = group == 0, group == 3
    for g in range(4):
        value = ext[g * MARGIN : (g + 1) * MARGIN, :TILE]
        turn = (-MARGIN * g) % TILE
        value = value + jnp.where(first, pltpu.roll(halo[2], turn, 1) if turn else halo[2], 0.0)
        turn = (MARGIN * (3 - g)) % TILE
        value = value + jnp.where(last, pltpu.roll(halo[3], turn, 1) if turn else halo[3], 0.0)
        if g == 0:
            value = value + halo[0]
            value = value + jnp.where(first, halo[4], 0.0) + jnp.where(last, pltpu.roll(halo[5], BS, 1), 0.0)
        if g == 3:
            value = value + halo[1]
            value = value + jnp.where(first, halo[6], 0.0) + jnp.where(last, pltpu.roll(halo[7], BS, 1), 0.0)
        out_grid[g * MARGIN : (g + 1) * MARGIN, :] = value

    @pl.when(even)
    def _():
        for copy in sends("even"):
            copy.wait_send()
        for d, j in ((1, 0), (1, 1), (1, 2), (2, 0), (2, 1)):
            for copy in relays("even", d, j):
                copy.wait_send()

    @pl.when(odd)
    def _():
        for copy in sends("odd"):
            copy.wait_send()
        for d, j in ((1, 0), (1, 1), (1, 2), (2, 0), (2, 1)):
            for copy in relays("odd", d, j):
                copy.wait_send()

    for copy in rims + late:
        copy.wait_send()


def solution(mesh):
    rows, cols = mesh.shape["row"], mesh.shape["col"]

    def shards(p2_panel, density, pattern, x_basis, x_offset, x_extent, y_basis, y_offset, y_extent):
        outside = pl.BlockSpec(memory_space=pltpu.HBM)
        inside = pl.BlockSpec(memory_space=pltpu.VMEM)
        new, grid = pl.pallas_call(
            functools.partial(kernel, rows, cols),
            out_shape=(
                jax.ShapeDtypeStruct((WC * BS, PANEL), BF16),
                jax.ShapeDtypeStruct((SX, TILE), F32),
            ),
            in_specs=[outside] * 9,
            out_specs=(inside, inside),
            scratch_shapes=[
                pltpu.VMEM((PANEL, W * BS), BF16),
                pltpu.VMEM((WC * BS, PANEL), BF16),
                pltpu.VMEM((BR, W), jnp.int32),
                pltpu.VMEM((32, PANEL), BF16),
                pltpu.VMEM((32, WC * BS), BF16),
                pltpu.SMEM((BR,), jnp.int32),
                pltpu.SMEM((BR,), jnp.int32),
                pltpu.SMEM((1, WC), jnp.int32),
                pltpu.SMEM((1, WC), jnp.int32),
                pltpu.VMEM((WC * BS, PANEL), BF16),
                pltpu.VMEM((IN_ROWS, PANEL), BF16),
                pltpu.VMEM((IN_ROWS, PANEL), BF16),
                pltpu.VMEM((WC * BS, PANEL), F32),
                pltpu.VMEM((CELLS, PANEL), BF16),
                pltpu.VMEM((2 * TILE, WC * BS), BF16),
                pltpu.VMEM((BR, PANEL), F32),
                pltpu.VMEM((CELLS, 2 * TILE), F32),
                pltpu.VMEM((2, MARGIN, TILE), F32),
                pltpu.VMEM((8, MARGIN, TILE), F32),
                pltpu.SemaphoreType.DMA((15,)),
                pltpu.SemaphoreType.DMA((16,)),
                pltpu.SemaphoreType.DMA((8,)),
                pltpu.SemaphoreType.DMA((8,)),
                pltpu.SemaphoreType.DMA((8,)),
                pltpu.SemaphoreType.DMA((8,)),
            ],
            compiler_params=pltpu.CompilerParams(
                collective_id=0, has_side_effects=True, vmem_limit_bytes=60 * 1024 * 1024
            ),
        )(
            p2_panel, density.T, pattern, x_basis.T, x_offset, x_extent, y_basis[0].T, y_offset, y_extent
        )
        return new.T, grid

    placed = (
        P("row", None),
        P("row", "col"),
        P("row", None),
        P("row", None),
        P("row"),
        P("row"),
        P("row", "col", None),
        P("row", "col"),
        P("row", "col"),
    )
    return jax.shard_map(
        shards,
        mesh=mesh,
        in_specs=placed,
        out_specs=(P("row", "col"), P("row", "col")),
        check_vma=False,
    )
```

```python
import functools

import jax
import jax.numpy as jnp
from jax import lax
from jax.experimental import pallas as pl
from jax.experimental.pallas import tpu as pltpu
from jax.sharding import PartitionSpec as P

MESH = pl.DeviceIdType.MESH
BS = 64
BR = 8
CLASSES = 8
WC = 7
W = 56
PANEL = 512
TILE = 128
CELLS = 192
SX = 128
MARGIN = 32
F32 = jnp.float32
BF16 = jnp.bfloat16

UP = {
    1: ((320, 128), (192, 128), (64, 128)),
    2: ((320, 128), (192, 128), (128, 64)),
    3: ((320, 128), (192, 128)),
}
DOWN = {
    1: ((0, 128), (128, 128), (256, 128)),
    2: ((0, 128), (128, 128), (256, 64)),
    3: ((0, 128), (128, 128)),
}
FIRST = {1: 0, 2: 3, 3: 6}
BASE = {1: 0, 2: 384, 3: 704}
IN_ROWS = 960


def dot_nt(left, right):
    return lax.dot_general(left, right, (((1,), (1,)), ((), ())), preferred_element_type=F32)


def kernel(
    rows, cols,
    p2, dens, pat, xb, xo, xe, yb, yo, ye,
    out_new, out_grid,
    s, dv, pv, xbv, ybv, xov, xev, yov, yev,
    own, up_in, down_in, acc, spread_x, spread_y, mask_rows, ext, packed, halo,
    load_sem, send_sem, up_sem, down_sem, hsend_sem, halo_sem,
):
    r = lax.axis_index("row")
    c = lax.axis_index("col")
    even = lax.rem(r, 2) == 0
    odd = lax.rem(r, 2) == 1

    def at(dr, dc):
        return (lax.rem(r + (dr + rows), rows), lax.rem(c + (dc + cols), cols))

    barrier = pltpu.get_barrier_semaphore()
    friends = [(-1, 0), (1, 0), (-2, 0), (2, 0), (0, -1), (0, 1), (-1, -1), (-1, 1), (1, -1), (1, 1)]
    for dr, dc in friends:
        pl.semaphore_signal(barrier, inc=1, device_id=at(dr, dc), device_id_type=MESH)

    loads = []
    for number, (source, target) in enumerate(
        ((dens, dv), (pat, pv), (xb, xbv), (yb, ybv), (xo, xov), (xe, xev), (yo, yov), (ye, yev))
    ):
        loads.append(pltpu.make_async_copy(source, target, load_sem.at[number]))
    square_loads = {}
    for number, block in enumerate((3, 2, 4, 1, 5, 0, 6)):
        part = pl.ds(block * PANEL, PANEL)
        square_loads[block] = pltpu.make_async_copy(p2.at[:, part], s.at[:, part], load_sem.at[8 + number])
    for load in loads:
        load.start()
    for block in (3, 2, 4, 1, 5, 0, 6):
        square_loads[block].start()

    loads[1].wait()
    pattern = pv[...].astype(F32).astype(BF16)
    position = lax.broadcasted_iota(jnp.int32, (BR, W), 1)
    slot = lax.broadcasted_iota(jnp.int32, (BR, W), 0)
    chosen = jnp.where(position == slot * CLASSES + c, 1.0, 0.0).astype(BF16)
    by_slot = dot_nt(chosen, pattern)
    block_row = lax.broadcasted_iota(jnp.int32, (BR, PANEL), 0)
    row_block = lax.broadcasted_iota(jnp.int32, (BR, PANEL), 1) // BS
    widen = jnp.where(block_row == row_block, 1.0, 0.0).astype(BF16)
    mask_rows[...] = jnp.dot(by_slot.astype(BF16), widen, preferred_element_type=F32)

    loads[0].wait()
    for k in range(WC):
        part = pl.ds(k * BS, BS)
        keep = jnp.broadcast_to(mask_rows[k : k + 1, :], (BS, PANEL)).astype(BF16)
        own[part, :] = dv[part, :] * keep

    pl.semaphore_wait(barrier, len(friends))

    def send(source, landing, sem, number, place):
        return pltpu.make_async_remote_copy(
            src_ref=source,
            dst_ref=landing,
            send_sem=send_sem.at[number],
            recv_sem=sem,
            device_id=place,
            device_id_type=MESH,
        )

    sides = {
        "even": (UP, up_in, up_sem, 1),
        "odd": (DOWN, down_in, down_sem, -1),
    }

    def landing(kind, d, chunk):
        first, count = chunk
        start = BASE[d] + first - (d * BS if kind == "even" else 0)
        return sides[kind][1].at[pl.ds(start, count)]

    def sends(kind):
        chunks, _, sem, sign = sides[kind]
        other = "odd" if kind == "even" else "even"
        other_chunks, _, other_sem, _ = sides[other]
        found = []
        for j in range(3):
            one, two = FIRST[1] + j, FIRST[2] + j
            far, near, back = chunks[2][j], chunks[1][j], other_chunks[1][j]
            found.append(send(own.at[pl.ds(*far)], landing(kind, 2, far), sem.at[two], 3 + j, at(2 * sign, 0)))
            found.append(send(own.at[pl.ds(*back)], landing(other, 1, back), other_sem.at[one], 6 + j, at(-sign, 0)))
            found.append(send(own.at[pl.ds(*near)], landing(kind, 1, near), sem.at[one], j, at(sign, 0)))
        return found

    @pl.when(even)
    def _():
        for copy in sends("even"):
            copy.start()

    @pl.when(odd)
    def _():
        for copy in sends("odd"):
            copy.start()

    def relays(kind, d, j):
        chunks, _, sem, sign = sides[kind]
        found = []

        def relay(to, number, place):
            chunk = chunks[to][j]
            found.append(
                send(landing(kind, d, chunk), landing(kind, to, chunk), sem.at[FIRST[to] + j], number, place)
            )

        if d == 1:
            if j < 2:
                relay(3, 9 + j, at(2 * sign, 0))
            relay(2, 11 + j, at(sign, 0))
        if d == 2 and j < 2:
            relay(3, 14 + j, at(sign, 0))
        return found

    def arrived(kind, d, j):
        chunks, _, sem, _ = sides[kind]
        place = landing(kind, d, chunks[d][j])
        send(place, place, sem.at[FIRST[d] + j], 0, at(-1, 0)).wait_recv()
        if d < 3:
            @pl.when(even if kind == "even" else odd)
            def _():
                for copy in relays(kind, d, j):
                    copy.start()

    position = lax.broadcasted_iota(jnp.int32, (W, PANEL), 0)
    natural = lax.broadcasted_iota(jnp.int32, (W, PANEL), 1) // BS
    for block in (3, 2, 4, 1, 5, 0, 6):
        square_loads[block].wait()
        chosen = jnp.where(position == natural + block * BR, 1.0, 0.0).astype(BF16)
        mask = jnp.dot(pattern, chosen, preferred_element_type=F32)
        for i in range(BR):
            keep = jnp.broadcast_to(mask[i : i + 1, :], (BS, PANEL)).astype(BF16)
            part = pl.ds(i * BS, BS)
            s[part, pl.ds(block * PANEL, PANEL)] = s[part, pl.ds(block * PANEL, PANEL)] * keep

    parity = lax.rem(c, 2)
    to_row = lax.broadcasted_iota(jnp.int32, (BS, TILE), 0)
    from_lane = lax.broadcasted_iota(jnp.int32, (BS, TILE), 1)
    pick = jnp.where(from_lane == to_row + parity * BS, -1.5, 0.0).astype(BF16)
    acc[...] = dot_nt(own[...], s[:, pl.ds(3 * PANEL, PANEL)])
    for k in range(WC):
        start = pl.multiple_of(k * PANEL + (c // 2) * TILE, TILE)
        part = pl.ds(k * BS, BS)
        acc[part, :] = acc[part, :] + dot_nt(pick, s[:, pl.ds(start, TILE)])

    def gather(kind, d, j):
        first, count = sides[kind][0][d][j]
        block = 3 - d if kind == "even" else 3 + d
        part = pl.ds(first - d * BS if kind == "even" else first + d * BS, count)
        place = landing(kind, d, (first, count))
        acc[part, :] = acc[part, :] + dot_nt(place[...], s[:, pl.ds(block * PANEL, PANEL)])

    for load in loads[2:]:
        load.wait()
    step_ids = lax.broadcasted_iota(jnp.int32, (2 * TILE, 32), 1)
    row_ids = lax.broadcasted_iota(jnp.int32, (2 * TILE, 32), 0)
    cell_ids = jnp.where(
        row_ids < CELLS - MARGIN, row_ids + MARGIN, jnp.where(row_ids < CELLS, row_ids - (CELLS - MARGIN), -1)
    )
    low = lax.broadcasted_iota(jnp.int32, (2 * TILE, TILE), 1) < BS

    def spread(values, offset, extent):
        hit = (cell_ids == offset + step_ids) & (step_ids < extent)
        onehot = jnp.where(hit, 1.0, 0.0).astype(BF16)
        return jnp.dot(onehot, values, preferred_element_type=F32)

    for t in range(4):
        part = pl.ds(t * TILE, TILE)
        pair = [spread(xbv[:, part], xov[2 * t + h], xev[2 * t + h]) for h in range(2)]
        spread_x[:, part] = jnp.where(low, pair[0], pair[1])[:CELLS].astype(BF16)
        if t < 3:
            pair = [spread(ybv[:, part], yov[0, 2 * t + h], yev[0, 2 * t + h]) for h in range(2)]
            spread_y[:, part] = jnp.where(low, pair[0], pair[1]).astype(BF16)
        else:
            part = pl.ds(t * TILE, BS)
            spread_y[:, part] = spread(ybv[:, part], yov[0, 6], yev[0, 6]).astype(BF16)

    for j in range(3):
        for d in (1, 2):
            for kind in ("even", "odd"):
                arrived(kind, d, j)
                gather(kind, d, j)
    for j in range(2):
        for kind in ("even", "odd"):
            arrived(kind, 3, j)
            gather(kind, 3, j)

    for k in range(WC):
        part = pl.ds(k * BS, BS)
        keep = jnp.broadcast_to(mask_rows[k : k + 1, :] * -2.0, (BS, PANEL))
        out_new[part, :] = (acc[part, :] * keep).astype(BF16)
    half_done = jnp.dot(spread_y[...], out_new[...], preferred_element_type=F32).astype(BF16)
    ext[SX:, :] = dot_nt(spread_x[SX:, :], half_done)

    def rim(number, source, place):
        return pltpu.make_async_remote_copy(
            src_ref=source,
            dst_ref=halo.at[number],
            send_sem=hsend_sem.at[number],
            recv_sem=halo_sem.at[number],
            device_id=place,
            device_id_type=MESH,
        )

    high_rows, low_rows = pl.ds(SX, MARGIN), pl.ds(SX + MARGIN, MARGIN)
    rims = [
        rim(4, ext.at[high_rows, pl.ds(TILE, TILE)], at(1, 1)),
        rim(5, ext.at[high_rows, pl.ds(TILE, TILE)], at(1, -1)),
        rim(6, ext.at[low_rows, pl.ds(TILE, TILE)], at(-1, 1)),
        rim(7, ext.at[low_rows, pl.ds(TILE, TILE)], at(-1, -1)),
        rim(0, ext.at[high_rows, pl.ds(0, TILE)], at(1, 0)),
        rim(1, ext.at[low_rows, pl.ds(0, TILE)], at(-1, 0)),
    ]
    for copy in rims:
        copy.start()
    ext[:SX, :] = dot_nt(spread_x[:SX, :], half_done)
    lane = lax.broadcasted_iota(jnp.int32, (MARGIN, TILE), 1)
    group = lane // MARGIN
    margins = [jnp.zeros((MARGIN, TILE), F32), jnp.zeros((MARGIN, TILE), F32)]
    for g in range(4):
        piece = ext[g * MARGIN : (g + 1) * MARGIN, TILE : 2 * TILE]
        for side in range(2):
            turn = (MARGIN * (g - side)) % TILE
            turned = pltpu.roll(piece, turn, 1) if turn else piece
            margins[side] = jnp.where(group == g, turned, margins[side])
    packed[0] = margins[0]
    packed[1] = margins[1]
    late = [rim(2, packed.at[0], at(0, 1)), rim(3, packed.at[1], at(0, -1))]
    for copy in late:
        copy.start()

    for number in (0, 1, 2, 3, 4, 5, 6, 7):
        rim(number, halo.at[number], at(1, 0)).wait_recv()
    first, last = group == 0, group == 3
    for g in range(4):
        value = ext[g * MARGIN : (g + 1) * MARGIN, :TILE]
        turn = (-MARGIN * g) % TILE
        value = value + jnp.where(first, pltpu.roll(halo[2], turn, 1) if turn else halo[2], 0.0)
        turn = (MARGIN * (3 - g)) % TILE
        value = value + jnp.where(last, pltpu.roll(halo[3], turn, 1) if turn else halo[3], 0.0)
        if g == 0:
            value = value + halo[0]
            value = value + jnp.where(first, halo[4], 0.0) + jnp.where(last, pltpu.roll(halo[5], BS, 1), 0.0)
        if g == 3:
            value = value + halo[1]
            value = value + jnp.where(first, halo[6], 0.0) + jnp.where(last, pltpu.roll(halo[7], BS, 1), 0.0)
        out_grid[g * MARGIN : (g + 1) * MARGIN, :] = value

    @pl.when(even)
    def _():
        for copy in sends("even"):
            copy.wait_send()
        for d, j in ((1, 0), (1, 1), (1, 2), (2, 0), (2, 1)):
            for copy in relays("even", d, j):
                copy.wait_send()

    @pl.when(odd)
    def _():
        for copy in sends("odd"):
            copy.wait_send()
        for d, j in ((1, 0), (1, 1), (1, 2), (2, 0), (2, 1)):
            for copy in relays("odd", d, j):
                copy.wait_send()

    for copy in rims + late:
        copy.wait_send()


def finish(new, grid, out_new, out_grid, sem):
    copies = [pltpu.make_async_copy(new, out_new, sem.at[0]), pltpu.make_async_copy(grid, out_grid, sem.at[1])]
    for copy in copies:
        copy.start()
    for copy in copies:
        copy.wait()


def solution(mesh):
    rows, cols = mesh.shape["row"], mesh.shape["col"]

    def shards(p2_panel, density, pattern, x_basis, x_offset, x_extent, y_basis, y_offset, y_extent):
        outside = pl.BlockSpec(memory_space=pltpu.HBM)
        inside = pl.BlockSpec(memory_space=pltpu.VMEM)
        new, grid = pl.pallas_call(
            functools.partial(kernel, rows, cols),
            out_shape=(pltpu.VMEM((WC * BS, PANEL), BF16), pltpu.VMEM((SX, TILE), F32)),
            in_specs=[outside] * 9,
            out_specs=(inside, inside),
            scratch_shapes=[
                pltpu.VMEM((PANEL, W * BS), BF16),
                pltpu.VMEM((WC * BS, PANEL), BF16),
                pltpu.VMEM((BR, W), jnp.int32),
                pltpu.VMEM((32, PANEL), BF16),
                pltpu.VMEM((32, WC * BS), BF16),
                pltpu.SMEM((BR,), jnp.int32),
                pltpu.SMEM((BR,), jnp.int32),
                pltpu.SMEM((1, WC), jnp.int32),
                pltpu.SMEM((1, WC), jnp.int32),
                pltpu.VMEM((WC * BS, PANEL), BF16),
                pltpu.VMEM((IN_ROWS, PANEL), BF16),
                pltpu.VMEM((IN_ROWS, PANEL), BF16),
                pltpu.VMEM((WC * BS, PANEL), F32),
                pltpu.VMEM((CELLS, PANEL), BF16),
                pltpu.VMEM((2 * TILE, WC * BS), BF16),
                pltpu.VMEM((BR, PANEL), F32),
                pltpu.VMEM((CELLS, 2 * TILE), F32),
                pltpu.VMEM((2, MARGIN, TILE), F32),
                pltpu.VMEM((8, MARGIN, TILE), F32),
                pltpu.SemaphoreType.DMA((15,)),
                pltpu.SemaphoreType.DMA((16,)),
                pltpu.SemaphoreType.DMA((8,)),
                pltpu.SemaphoreType.DMA((8,)),
                pltpu.SemaphoreType.DMA((8,)),
                pltpu.SemaphoreType.DMA((8,)),
            ],
            compiler_params=pltpu.CompilerParams(
                collective_id=0, has_side_effects=True, vmem_limit_bytes=62914560
            ),
        )(
            p2_panel, density.T, pattern, x_basis.T, x_offset, x_extent, y_basis[0].T, y_offset, y_extent
        )
        new, grid = pl.pallas_call(
            finish,
            out_shape=(
                jax.ShapeDtypeStruct((WC * BS, PANEL), BF16),
                jax.ShapeDtypeStruct((SX, TILE), F32),
            ),
            in_specs=[inside, inside],
            out_specs=(outside, outside),
            scratch_shapes=[pltpu.SemaphoreType.DMA((2,))],
            compiler_params=pltpu.CompilerParams(vmem_limit_bytes=4 * 1024 * 1024),
        )(new, grid)
        return new.T, grid

    placed = (
        P("row", None),
        P("row", "col"),
        P("row", None),
        P("row", None),
        P("row"),
        P("row"),
        P("row", "col", None),
        P("row", "col"),
        P("row", "col"),
    )
    return jax.shard_map(
        shards,
        mesh=mesh,
        in_specs=placed,
        out_specs=(P("row", "col"), P("row", "col")),
        check_vma=False,
    )
```

```python
import functools

import jax
import jax.numpy as jnp
from jax import lax
from jax.experimental import pallas as pl
from jax.experimental.pallas import tpu as pltpu
from jax.sharding import PartitionSpec as P

MESH = pl.DeviceIdType.MESH
BS = 64
BR = 8
CLASSES = 8
WC = 7
W = 56
PANEL = 512
TILE = 128
CELLS = 192
SX = 128
MARGIN = 32
F32 = jnp.float32
BF16 = jnp.bfloat16

UP = {
    1: ((320, 128), (192, 128), (64, 128)),
    2: ((320, 128), (192, 128), (128, 64)),
    3: ((320, 128), (192, 128)),
}
DOWN = {
    1: ((0, 128), (128, 128), (256, 128)),
    2: ((0, 128), (128, 128), (256, 64)),
    3: ((0, 128), (128, 128)),
}
FIRST = {1: 0, 2: 3, 3: 6}
BASE = {1: 0, 2: 384, 3: 704}
IN_ROWS = 960


def dot_nt(left, right):
    return lax.dot_general(left, right, (((1,), (1,)), ((), ())), preferred_element_type=F32)


def kernel(
    rows, cols,
    p2, dens, pat, xb, xo, xe, yb, yo, ye,
    out_new, out_grid,
    s, dv, pv, xbv, ybv, xov, xev, yov, yev,
    own, up_in, down_in, acc, spread_x, spread_y, mask_rows, ext, packed, halo,
    load_sem, send_sem, up_sem, down_sem, hsend_sem, halo_sem,
):
    r = lax.axis_index("row")
    c = lax.axis_index("col")
    even = lax.rem(r, 2) == 0
    odd = lax.rem(r, 2) == 1

    def at(dr, dc):
        return (lax.rem(r + (dr + rows), rows), lax.rem(c + (dc + cols), cols))

    barrier = pltpu.get_barrier_semaphore()
    friends = [(-1, 0), (1, 0), (-2, 0), (2, 0), (0, -1), (0, 1), (-1, -1), (-1, 1), (1, -1), (1, 1)]
    for dr, dc in friends:
        pl.semaphore_signal(barrier, inc=1, device_id=at(dr, dc), device_id_type=MESH)

    loads = []
    for number, (source, target) in enumerate(
        ((dens, dv), (pat, pv), (xb, xbv), (yb, ybv), (xo, xov), (xe, xev), (yo, yov), (ye, yev))
    ):
        loads.append(pltpu.make_async_copy(source, target, load_sem.at[number]))
    square_loads = {}
    for number, block in enumerate((3, 2, 4, 1, 5, 0, 6)):
        part = pl.ds(block * PANEL, PANEL)
        square_loads[block] = pltpu.make_async_copy(p2.at[:, part], s.at[:, part], load_sem.at[8 + number])
    for load in loads:
        load.start()
    for block in (3, 2, 4, 1, 5, 0, 6):
        square_loads[block].start()

    loads[1].wait()
    pattern = pv[...].astype(F32).astype(BF16)
    position = lax.broadcasted_iota(jnp.int32, (BR, W), 1)
    slot = lax.broadcasted_iota(jnp.int32, (BR, W), 0)
    chosen = jnp.where(position == slot * CLASSES + c, 1.0, 0.0).astype(BF16)
    by_slot = dot_nt(chosen, pattern)
    block_row = lax.broadcasted_iota(jnp.int32, (BR, PANEL), 0)
    row_block = lax.broadcasted_iota(jnp.int32, (BR, PANEL), 1) // BS
    widen = jnp.where(block_row == row_block, 1.0, 0.0).astype(BF16)
    mask_rows[...] = jnp.dot(by_slot.astype(BF16), widen, preferred_element_type=F32)

    loads[0].wait()
    for k in range(WC):
        part = pl.ds(k * BS, BS)
        keep = jnp.broadcast_to(mask_rows[k : k + 1, :], (BS, PANEL)).astype(BF16)
        own[part, :] = dv[part, :] * keep

    pl.semaphore_wait(barrier, len(friends))

    def send(source, landing, sem, number, place):
        return pltpu.make_async_remote_copy(
            src_ref=source,
            dst_ref=landing,
            send_sem=send_sem.at[number],
            recv_sem=sem,
            device_id=place,
            device_id_type=MESH,
        )

    sides = {
        "even": (UP, up_in, up_sem, 1),
        "odd": (DOWN, down_in, down_sem, -1),
    }

    def landing(kind, d, chunk):
        first, count = chunk
        start = BASE[d] + first - (d * BS if kind == "even" else 0)
        return sides[kind][1].at[pl.ds(start, count)]

    def sends(kind):
        chunks, _, sem, sign = sides[kind]
        other = "odd" if kind == "even" else "even"
        other_chunks, _, other_sem, _ = sides[other]
        found = []
        for j in range(3):
            one, two = FIRST[1] + j, FIRST[2] + j
            far, near, back = chunks[2][j], chunks[1][j], other_chunks[1][j]
            found.append(send(own.at[pl.ds(*far)], landing(kind, 2, far), sem.at[two], 3 + j, at(2 * sign, 0)))
            found.append(send(own.at[pl.ds(*back)], landing(other, 1, back), other_sem.at[one], 6 + j, at(-sign, 0)))
            found.append(send(own.at[pl.ds(*near)], landing(kind, 1, near), sem.at[one], j, at(sign, 0)))
        return found

    @pl.when(even)
    def _():
        for copy in sends("even"):
            copy.start()

    @pl.when(odd)
    def _():
        for copy in sends("odd"):
            copy.start()

    def relays(kind, d, j):
        chunks, _, sem, sign = sides[kind]
        found = []

        def relay(to, number, place):
            chunk = chunks[to][j]
            found.append(
                send(landing(kind, d, chunk), landing(kind, to, chunk), sem.at[FIRST[to] + j], number, place)
            )

        if d == 1:
            if j < 2:
                relay(3, 9 + j, at(2 * sign, 0))
            relay(2, 11 + j, at(sign, 0))
        if d == 2 and j < 2:
            relay(3, 14 + j, at(sign, 0))
        return found

    def arrived(mine, kind, d, j):
        chunks, _, sem, _ = sides[kind]
        place = landing(kind, d, chunks[d][j])
        send(place, place, sem.at[FIRST[d] + j], 0, at(-1, 0)).wait_recv()
        if d < 3 and kind == mine:
            for copy in relays(kind, d, j):
                copy.start()

    position = lax.broadcasted_iota(jnp.int32, (W, PANEL), 0)
    natural = lax.broadcasted_iota(jnp.int32, (W, PANEL), 1) // BS
    for block in (3, 2, 4, 1, 5, 0, 6):
        square_loads[block].wait()
        chosen = jnp.where(position == natural + block * BR, 1.0, 0.0).astype(BF16)
        mask = jnp.dot(pattern, chosen, preferred_element_type=F32)
        for i in range(BR):
            keep = jnp.broadcast_to(mask[i : i + 1, :], (BS, PANEL)).astype(BF16)
            part = pl.ds(i * BS, BS)
            s[part, pl.ds(block * PANEL, PANEL)] = s[part, pl.ds(block * PANEL, PANEL)] * keep

    parity = lax.rem(c, 2)
    to_row = lax.broadcasted_iota(jnp.int32, (BS, TILE), 0)
    from_lane = lax.broadcasted_iota(jnp.int32, (BS, TILE), 1)
    pick = jnp.where(from_lane == to_row + parity * BS, -1.5, 0.0).astype(BF16)
    acc[...] = dot_nt(own[...], s[:, pl.ds(3 * PANEL, PANEL)])
    for k in range(WC):
        start = pl.multiple_of(k * PANEL + (c // 2) * TILE, TILE)
        part = pl.ds(k * BS, BS)
        acc[part, :] = acc[part, :] + dot_nt(pick, s[:, pl.ds(start, TILE)])

    def gather(kind, d, parts):
        chunks = [sides[kind][0][d][j] for j in parts]
        first = min(chunk[0] for chunk in chunks)
        count = sum(chunk[1] for chunk in chunks)
        block = 3 - d if kind == "even" else 3 + d
        part = pl.ds(first - d * BS if kind == "even" else first + d * BS, count)
        place = landing(kind, d, (first, count))
        acc[part, :] = acc[part, :] + dot_nt(place[...], s[:, pl.ds(block * PANEL, PANEL)])

    for load in loads[2:]:
        load.wait()
    step_ids = lax.broadcasted_iota(jnp.int32, (2 * TILE, 32), 1)
    row_ids = lax.broadcasted_iota(jnp.int32, (2 * TILE, 32), 0)
    cell_ids = jnp.where(
        row_ids < CELLS - MARGIN, row_ids + MARGIN, jnp.where(row_ids < CELLS, row_ids - (CELLS - MARGIN), -1)
    )
    low = lax.broadcasted_iota(jnp.int32, (2 * TILE, TILE), 1) < BS

    def spread(values, offset, extent):
        hit = (cell_ids == offset + step_ids) & (step_ids < extent)
        onehot = jnp.where(hit, 1.0, 0.0).astype(BF16)
        return jnp.dot(onehot, values, preferred_element_type=F32)

    for t in range(4):
        part = pl.ds(t * TILE, TILE)
        pair = [spread(xbv[:, part], xov[2 * t + h], xev[2 * t + h]) for h in range(2)]
        spread_x[:, part] = jnp.where(low, pair[0], pair[1])[:CELLS].astype(BF16)
        if t < 3:
            pair = [spread(ybv[:, part], yov[0, 2 * t + h], yev[0, 2 * t + h]) for h in range(2)]
            spread_y[:, part] = jnp.where(low, pair[0], pair[1]).astype(BF16)
        else:
            part = pl.ds(t * TILE, BS)
            spread_y[:, part] = spread(ybv[:, part], yov[0, 6], yev[0, 6]).astype(BF16)

    def collect(mine):
        theirs = "odd" if mine == "even" else "even"
        steps = (
            (theirs, 1, (0, 1, 2)), (mine, 1, (0,)), (mine, 2, (0,)), (mine, 1, (1,)), (mine, 2, (1,)),
            (theirs, 2, (0, 1)), (theirs, 3, (0, 1)), (mine, 2, (2,)), (mine, 1, (2,)), (theirs, 2, (2,)),
            (mine, 3, (0,)), (mine, 3, (1,)),
        )
        for kind, d, parts in steps:
            for j in parts:
                arrived(mine, kind, d, j)
            gather(kind, d, parts)

    @pl.when(even)
    def _():
        collect("even")

    @pl.when(odd)
    def _():
        collect("odd")

    for k in range(WC):
        part = pl.ds(k * BS, BS)
        keep = jnp.broadcast_to(mask_rows[k : k + 1, :] * -2.0, (BS, PANEL))
        out_new[part, :] = (acc[part, :] * keep).astype(BF16)
    half_done = jnp.dot(spread_y[...], out_new[...], preferred_element_type=F32).astype(BF16)
    ext[SX:, :] = dot_nt(spread_x[SX:, :], half_done)

    def rim(number, source, place):
        return pltpu.make_async_remote_copy(
            src_ref=source,
            dst_ref=halo.at[number],
            send_sem=hsend_sem.at[number],
            recv_sem=halo_sem.at[number],
            device_id=place,
            device_id_type=MESH,
        )

    high_rows, low_rows = pl.ds(SX, MARGIN), pl.ds(SX + MARGIN, MARGIN)
    rims = [
        rim(4, ext.at[high_rows, pl.ds(TILE, TILE)], at(1, 1)),
        rim(5, ext.at[high_rows, pl.ds(TILE, TILE)], at(1, -1)),
        rim(6, ext.at[low_rows, pl.ds(TILE, TILE)], at(-1, 1)),
        rim(7, ext.at[low_rows, pl.ds(TILE, TILE)], at(-1, -1)),
        rim(0, ext.at[high_rows, pl.ds(0, TILE)], at(1, 0)),
        rim(1, ext.at[low_rows, pl.ds(0, TILE)], at(-1, 0)),
    ]
    for copy in rims:
        copy.start()
    ext[:SX, :] = dot_nt(spread_x[:SX, :], half_done)
    lane = lax.broadcasted_iota(jnp.int32, (MARGIN, TILE), 1)
    group = lane // MARGIN
    margins = [jnp.zeros((MARGIN, TILE), F32), jnp.zeros((MARGIN, TILE), F32)]
    for g in range(4):
        piece = ext[g * MARGIN : (g + 1) * MARGIN, TILE : 2 * TILE]
        for side in range(2):
            turn = (MARGIN * (g - side)) % TILE
            turned = pltpu.roll(piece, turn, 1) if turn else piece
            margins[side] = jnp.where(group == g, turned, margins[side])
    packed[0] = margins[0]
    packed[1] = margins[1]
    late = [rim(2, packed.at[0], at(0, 1)), rim(3, packed.at[1], at(0, -1))]
    for copy in late:
        copy.start()

    for number in (0, 1, 2, 3, 4, 5, 6, 7):
        rim(number, halo.at[number], at(1, 0)).wait_recv()
    first, last = group == 0, group == 3
    for g in range(4):
        value = ext[g * MARGIN : (g + 1) * MARGIN, :TILE]
        turn = (-MARGIN * g) % TILE
        value = value + jnp.where(first, pltpu.roll(halo[2], turn, 1) if turn else halo[2], 0.0)
        turn = (MARGIN * (3 - g)) % TILE
        value = value + jnp.where(last, pltpu.roll(halo[3], turn, 1) if turn else halo[3], 0.0)
        if g == 0:
            value = value + halo[0]
            value = value + jnp.where(first, halo[4], 0.0) + jnp.where(last, pltpu.roll(halo[5], BS, 1), 0.0)
        if g == 3:
            value = value + halo[1]
            value = value + jnp.where(first, halo[6], 0.0) + jnp.where(last, pltpu.roll(halo[7], BS, 1), 0.0)
        out_grid[g * MARGIN : (g + 1) * MARGIN, :] = value

    @pl.when(even)
    def _():
        for copy in sends("even"):
            copy.wait_send()
        for d, j in ((1, 0), (1, 1), (1, 2), (2, 0), (2, 1)):
            for copy in relays("even", d, j):
                copy.wait_send()

    @pl.when(odd)
    def _():
        for copy in sends("odd"):
            copy.wait_send()
        for d, j in ((1, 0), (1, 1), (1, 2), (2, 0), (2, 1)):
            for copy in relays("odd", d, j):
                copy.wait_send()

    for copy in rims + late:
        copy.wait_send()


def finish(new, grid, out_new, out_grid, sem):
    copies = [pltpu.make_async_copy(new, out_new, sem.at[0]), pltpu.make_async_copy(grid, out_grid, sem.at[1])]
    for copy in copies:
        copy.start()
    for copy in copies:
        copy.wait()


def solution(mesh):
    rows, cols = mesh.shape["row"], mesh.shape["col"]

    def shards(p2_panel, density, pattern, x_basis, x_offset, x_extent, y_basis, y_offset, y_extent):
        outside = pl.BlockSpec(memory_space=pltpu.HBM)
        inside = pl.BlockSpec(memory_space=pltpu.VMEM)
        new, grid = pl.pallas_call(
            functools.partial(kernel, rows, cols),
            out_shape=(pltpu.VMEM((WC * BS, PANEL), BF16), pltpu.VMEM((SX, TILE), F32)),
            in_specs=[outside] * 9,
            out_specs=(inside, inside),
            scratch_shapes=[
                pltpu.VMEM((PANEL, W * BS), BF16),
                pltpu.VMEM((WC * BS, PANEL), BF16),
                pltpu.VMEM((BR, W), jnp.int32),
                pltpu.VMEM((32, PANEL), BF16),
                pltpu.VMEM((32, WC * BS), BF16),
                pltpu.SMEM((BR,), jnp.int32),
                pltpu.SMEM((BR,), jnp.int32),
                pltpu.SMEM((1, WC), jnp.int32),
                pltpu.SMEM((1, WC), jnp.int32),
                pltpu.VMEM((WC * BS, PANEL), BF16),
                pltpu.VMEM((IN_ROWS, PANEL), BF16),
                pltpu.VMEM((IN_ROWS, PANEL), BF16),
                pltpu.VMEM((WC * BS, PANEL), F32),
                pltpu.VMEM((CELLS, PANEL), BF16),
                pltpu.VMEM((2 * TILE, WC * BS), BF16),
                pltpu.VMEM((BR, PANEL), F32),
                pltpu.VMEM((CELLS, 2 * TILE), F32),
                pltpu.VMEM((2, MARGIN, TILE), F32),
                pltpu.VMEM((8, MARGIN, TILE), F32),
                pltpu.SemaphoreType.DMA((15,)),
                pltpu.SemaphoreType.DMA((16,)),
                pltpu.SemaphoreType.DMA((8,)),
                pltpu.SemaphoreType.DMA((8,)),
                pltpu.SemaphoreType.DMA((8,)),
                pltpu.SemaphoreType.DMA((8,)),
            ],
            compiler_params=pltpu.CompilerParams(
                collective_id=0, has_side_effects=True, vmem_limit_bytes=62914560
            ),
        )(
            p2_panel, density.T, pattern, x_basis.T, x_offset, x_extent, y_basis[0].T, y_offset, y_extent
        )
        new, grid = pl.pallas_call(
            finish,
            out_shape=(
                jax.ShapeDtypeStruct((WC * BS, PANEL), BF16),
                jax.ShapeDtypeStruct((SX, TILE), F32),
            ),
            in_specs=[inside, inside],
            out_specs=(outside, outside),
            scratch_shapes=[pltpu.SemaphoreType.DMA((2,))],
            compiler_params=pltpu.CompilerParams(vmem_limit_bytes=4 * 1024 * 1024),
        )(new, grid)
        return new.T, grid

    placed = (
        P("row", None),
        P("row", "col"),
        P("row", None),
        P("row", None),
        P("row"),
        P("row"),
        P("row", "col", None),
        P("row", "col"),
        P("row", "col"),
    )
    return jax.shard_map(
        shards,
        mesh=mesh,
        in_specs=placed,
        out_specs=(P("row", "col"), P("row", "col")),
        check_vma=False,
    )
```

```python
import functools

import jax
import jax.numpy as jnp
from jax import lax
from jax.experimental import pallas as pl
from jax.experimental.pallas import tpu as pltpu
from jax.sharding import PartitionSpec as P

MESH = pl.DeviceIdType.MESH
BS = 64
BR = 8
CLASSES = 8
WC = 7
W = 56
PANEL = 512
TILE = 128
CELLS = 192
SX = 128
MARGIN = 32
F32 = jnp.float32
BF16 = jnp.bfloat16

UP = {
    1: ((320, 128), (192, 128), (64, 128)),
    2: ((320, 128), (192, 128), (128, 64)),
    3: ((320, 128), (192, 128)),
}
DOWN = {
    1: ((0, 128), (128, 128), (256, 128)),
    2: ((0, 128), (128, 128), (256, 64)),
    3: ((0, 128), (128, 128)),
}
FIRST = {1: 0, 2: 3, 3: 6}
BASE = {1: 0, 2: 384, 3: 704}
IN_ROWS = 960


def dot_nt(left, right):
    return lax.dot_general(left, right, (((1,), (1,)), ((), ())), preferred_element_type=F32)


def kernel(
    rows, cols,
    p2, dens, pat, xb, xo, xe, yb, yo, ye,
    out_new, out_grid,
    s, dv, pv, xbv, ybv, xov, xev, yov, yev,
    own, up_in, down_in, acc, spread_x, spread_y, mask_rows, ext, packed, halo, corner_out, corner_in, half_part, half,
    load_sem, send_sem, up_sem, down_sem, hsend_sem, halo_sem, ready_sem,
):
    r = lax.axis_index("row")
    c = lax.axis_index("col")
    even = lax.rem(r, 2) == 0
    odd = lax.rem(r, 2) == 1

    def at(dr, dc):
        return (lax.rem(r + (dr + rows), rows), lax.rem(c + (dc + cols), cols))

    barrier = pltpu.get_barrier_semaphore()
    along_row = [(-1, 0), (1, 0), (-2, 0), (2, 0)]
    aside = [(0, -1), (0, 1), (-1, -1), (1, 1), (-1, 1), (1, -1)]
    for dr, dc in along_row:
        pl.semaphore_signal(barrier, inc=1, device_id=at(dr, dc), device_id_type=MESH)
    before = len(along_row)
    for dr, dc in aside:
        other = at(dr, dc)
        before = before + jnp.where(other[1] < c, 1, 0)

        @pl.when(other[1] > c)
        def _():
            pl.semaphore_signal(barrier, inc=1, device_id=other, device_id_type=MESH)

    loads = []
    for number, (source, target) in enumerate(
        ((dens, dv), (pat, pv), (xb, xbv), (yb, ybv), (xo, xov), (xe, xev), (yo, yov), (ye, yev))
    ):
        loads.append(pltpu.make_async_copy(source, target, load_sem.at[number]))
    square_loads = {}
    for number, block in enumerate((3, 2, 4, 1, 5, 0, 6)):
        part = pl.ds(block * PANEL, PANEL)
        square_loads[block] = pltpu.make_async_copy(p2.at[:, part], s.at[:, part], load_sem.at[8 + number])
    for load in loads:
        load.start()
    for block in (3, 2, 4, 1, 5, 0, 6):
        square_loads[block].start()

    loads[1].wait()
    pattern = pv[...].astype(F32).astype(BF16)
    position = lax.broadcasted_iota(jnp.int32, (BR, W), 1)
    slot = lax.broadcasted_iota(jnp.int32, (BR, W), 0)
    chosen = jnp.where(position == slot * CLASSES + c, 1.0, 0.0).astype(BF16)
    by_slot = dot_nt(chosen, pattern)
    block_row = lax.broadcasted_iota(jnp.int32, (BR, PANEL), 0)
    row_block = lax.broadcasted_iota(jnp.int32, (BR, PANEL), 1) // BS
    widen = jnp.where(block_row == row_block, 1.0, 0.0).astype(BF16)
    mask_rows[...] = jnp.dot(by_slot.astype(BF16), widen, preferred_element_type=F32)

    loads[0].wait()
    for k in range(WC):
        part = pl.ds(k * BS, BS)
        keep = jnp.broadcast_to(mask_rows[k : k + 1, :], (BS, PANEL)).astype(BF16)
        own[part, :] = dv[part, :] * keep

    pl.semaphore_wait(barrier, before)

    def send(source, landing, sem, number, place):
        return pltpu.make_async_remote_copy(
            src_ref=source,
            dst_ref=landing,
            send_sem=send_sem.at[number],
            recv_sem=sem,
            device_id=place,
            device_id_type=MESH,
        )

    sides = {
        "even": (UP, up_in, up_sem, 1),
        "odd": (DOWN, down_in, down_sem, -1),
    }

    def landing(kind, d, chunk):
        first, count = chunk
        start = BASE[d] + first - (d * BS if kind == "even" else 0)
        return sides[kind][1].at[pl.ds(start, count)]

    def sends(kind):
        chunks, _, sem, sign = sides[kind]
        other = "odd" if kind == "even" else "even"
        other_chunks, _, other_sem, _ = sides[other]
        found = []
        for j in range(3):
            one, two = FIRST[1] + j, FIRST[2] + j
            far, near, back = chunks[2][j], chunks[1][j], other_chunks[1][j]
            found.append(send(own.at[pl.ds(*far)], landing(kind, 2, far), sem.at[two], 3 + j, at(2 * sign, 0)))
            found.append(send(own.at[pl.ds(*back)], landing(other, 1, back), other_sem.at[one], 6 + j, at(-sign, 0)))
            found.append(send(own.at[pl.ds(*near)], landing(kind, 1, near), sem.at[one], j, at(sign, 0)))
        return found

    @pl.when(even)
    def _():
        for copy in sends("even"):
            copy.start()

    @pl.when(odd)
    def _():
        for copy in sends("odd"):
            copy.start()

    for number, (dr, dc) in enumerate(aside):
        other = at(dr, dc)

        @pl.when(other[1] < c)
        def _():
            pl.semaphore_signal(ready_sem.at[number ^ 1], inc=1, device_id=other, device_id_type=MESH)

    def relays(kind, d, j):
        chunks, _, sem, sign = sides[kind]
        found = []

        def relay(to, number, place):
            chunk = chunks[to][j]
            found.append(
                send(landing(kind, d, chunk), landing(kind, to, chunk), sem.at[FIRST[to] + j], number, place)
            )

        if d == 1:
            if j < 2:
                relay(3, 9 + j, at(2 * sign, 0))
            relay(2, 11 + j, at(sign, 0))
        if d == 2 and j < 2:
            relay(3, 14 + j, at(sign, 0))
        return found

    def arrived(mine, kind, d, j):
        chunks, _, sem, _ = sides[kind]
        place = landing(kind, d, chunks[d][j])
        send(place, place, sem.at[FIRST[d] + j], 0, at(-1, 0)).wait_recv()
        if d < 3 and kind == mine:
            for copy in relays(kind, d, j):
                copy.start()

    position = lax.broadcasted_iota(jnp.int32, (W, PANEL), 0)
    natural = lax.broadcasted_iota(jnp.int32, (W, PANEL), 1) // BS
    for block in (3, 2, 4, 1, 5, 0, 6):
        square_loads[block].wait()
        chosen = jnp.where(position == natural + block * BR, 1.0, 0.0).astype(BF16)
        mask = jnp.dot(pattern, chosen, preferred_element_type=F32)
        for i in range(BR):
            keep = jnp.broadcast_to(mask[i : i + 1, :], (BS, PANEL)).astype(BF16)
            part = pl.ds(i * BS, BS)
            s[part, pl.ds(block * PANEL, PANEL)] = s[part, pl.ds(block * PANEL, PANEL)] * keep

    parity = lax.rem(c, 2)
    to_row = lax.broadcasted_iota(jnp.int32, (BS, TILE), 0)
    from_lane = lax.broadcasted_iota(jnp.int32, (BS, TILE), 1)
    pick = jnp.where(from_lane == to_row + parity * BS, -1.5, 0.0).astype(BF16)
    acc[...] = dot_nt(own[...], s[:, pl.ds(3 * PANEL, PANEL)])
    for k in range(WC):
        start = pl.multiple_of(k * PANEL + (c // 2) * TILE, TILE)
        part = pl.ds(k * BS, BS)
        acc[part, :] = acc[part, :] + dot_nt(pick, s[:, pl.ds(start, TILE)])

    def gather(kind, d, parts):
        chunks = [sides[kind][0][d][j] for j in parts]
        first = min(chunk[0] for chunk in chunks)
        count = sum(chunk[1] for chunk in chunks)
        block = 3 - d if kind == "even" else 3 + d
        part = pl.ds(first - d * BS if kind == "even" else first + d * BS, count)
        place = landing(kind, d, (first, count))
        acc[part, :] = acc[part, :] + dot_nt(place[...], s[:, pl.ds(block * PANEL, PANEL)])

    for load in loads[2:]:
        load.wait()
    step_ids = lax.broadcasted_iota(jnp.int32, (2 * TILE, 32), 1)
    row_ids = lax.broadcasted_iota(jnp.int32, (2 * TILE, 32), 0)
    cell_ids = jnp.where(
        row_ids < CELLS - MARGIN, row_ids + MARGIN, jnp.where(row_ids < CELLS, row_ids - (CELLS - MARGIN), -1)
    )
    low = lax.broadcasted_iota(jnp.int32, (2 * TILE, TILE), 1) < BS

    def spread(values, offset, extent):
        hit = (cell_ids == offset + step_ids) & (step_ids < extent)
        onehot = jnp.where(hit, 1.0, 0.0).astype(BF16)
        return jnp.dot(onehot, values, preferred_element_type=F32)

    for t in range(4):
        part = pl.ds(t * TILE, TILE)
        pair = [spread(xbv[:, part], xov[2 * t + h], xev[2 * t + h]) for h in range(2)]
        spread_x[:, part] = jnp.where(low, pair[0], pair[1])[:CELLS].astype(BF16)
        if t < 3:
            pair = [spread(ybv[:, part], yov[0, 2 * t + h], yev[0, 2 * t + h]) for h in range(2)]
            spread_y[:, part] = jnp.where(low, pair[0], pair[1]).astype(BF16)
        else:
            part = pl.ds(t * TILE, BS)
            spread_y[:, part] = spread(ybv[:, part], yov[0, 6], yev[0, 6]).astype(BF16)

    def finish_rows(first, count):
        for k in range(first // BS, (first + count) // BS):
            part = pl.ds(k * BS, BS)
            keep = jnp.broadcast_to(mask_rows[k : k + 1, :] * -2.0, (BS, PANEL))
            out_new[part, :] = (acc[part, :] * keep).astype(BF16)
        part = pl.ds(first, count)
        return jnp.dot(spread_y[:, part], out_new[part, :], preferred_element_type=F32)

    def collect(mine):
        theirs = "odd" if mine == "even" else "even"
        steps = (
            (theirs, 1, (0, 1, 2)), (mine, 1, (0,)), (mine, 2, (0,)), (mine, 1, (1,)), (mine, 2, (1,)),
            (theirs, 2, (0, 1)), (theirs, 3, (0, 1)), (mine, 2, (2,)), (mine, 1, (2,)), (theirs, 2, (2,)),
            (mine, 3, (0,)), (mine, 3, (1,)),
        )
        early, late = ((128, 320), (0, 128)) if mine == "even" else ((0, 256), (256, 192))
        for number, (kind, d, parts) in enumerate(steps):
            if number == len(steps) - 1:
                half_part[...] = finish_rows(*early)
            for j in parts:
                arrived(mine, kind, d, j)
            gather(kind, d, parts)
        half[...] = (half_part[...] + finish_rows(*late)).astype(BF16)

    @pl.when(even)
    def _():
        collect("even")

    @pl.when(odd)
    def _():
        collect("odd")

    for number, (dr, dc) in enumerate(aside):
        @pl.when(at(dr, dc)[1] > c)
        def _():
            pl.semaphore_wait(ready_sem.at[number], 1)

    half_done = half[...]
    ext[SX:, :] = dot_nt(spread_x[SX:, :], half_done)

    def rim(number, source, place, box, slot):
        return pltpu.make_async_remote_copy(
            src_ref=source,
            dst_ref=box.at[slot],
            send_sem=hsend_sem.at[number],
            recv_sem=halo_sem.at[number],
            device_id=place,
            device_id_type=MESH,
        )

    rims = [
        rim(0, ext.at[pl.ds(SX, MARGIN), pl.ds(0, TILE)], at(1, 0), halo, 0),
        rim(1, ext.at[pl.ds(SX + MARGIN, MARGIN), pl.ds(0, TILE)], at(-1, 0), halo, 1),
    ]
    for copy in rims:
        copy.start()

    def pack(first_row, height, side):
        group = lax.broadcasted_iota(jnp.int32, (height, TILE), 1) // MARGIN
        joined = jnp.zeros((height, TILE), F32)
        for g in range(4):
            start = first_row + g * height
            piece = ext[start : start + height, TILE : 2 * TILE]
            turn = (MARGIN * (g - side)) % TILE
            joined = jnp.where(group == g, pltpu.roll(piece, turn, 1) if turn else piece, joined)
        return joined

    def unpack(value, g, side):
        turn = (MARGIN * (3 - g)) % TILE if side else (-MARGIN * g) % TILE
        value = pltpu.roll(value, turn, 1) if turn else value
        group = lax.broadcasted_iota(jnp.int32, value.shape, 1) // MARGIN
        return jnp.where(group == (3 if side else 0), value, 0.0)

    for number, (dr, dc) in enumerate(((1, 1), (1, -1), (-1, 1), (-1, -1))):
        corner_out[number] = pack(SX if dr > 0 else SX + MARGIN, MARGIN // 4, 0 if dc > 0 else 1)
        rims.append(rim(4 + number, corner_out.at[number], at(dr, dc), corner_in, number))
        rims[-1].start()
    ext[:SX, :] = dot_nt(spread_x[:SX, :], half_done)
    for number, dc in enumerate((1, -1)):
        packed[number] = pack(0, MARGIN, number)
        rims.append(rim(2 + number, packed.at[number], at(0, dc), halo, 2 + number))
        rims[-1].start()

    for number in range(4):
        rim(number, halo.at[number], at(1, 0), halo, number).wait_recv()
    for g in range(4):
        value = ext[g * MARGIN : (g + 1) * MARGIN, :TILE]
        value = value + unpack(halo[2], g, 0) + unpack(halo[3], g, 1)
        if g in (0, 3):
            value = value + halo[0 if g == 0 else 1]
        out_grid[g * MARGIN : (g + 1) * MARGIN, :] = value
    for number in range(4):
        rim(4 + number, corner_in.at[number], at(1, 0), corner_in, number).wait_recv()
    height = MARGIN // 4
    for start, pair in ((0, (0, 1)), (SX - MARGIN, (2, 3))):
        for g in range(4):
            part = pl.ds(start + g * height, height)
            rest = unpack(corner_in[pair[0]], g, 0) + unpack(corner_in[pair[1]], g, 1)
            out_grid[part, :] = out_grid[part, :] + rest

    @pl.when(even)
    def _():
        for copy in sends("even"):
            copy.wait_send()
        for d, j in ((1, 0), (1, 1), (1, 2), (2, 0), (2, 1)):
            for copy in relays("even", d, j):
                copy.wait_send()

    @pl.when(odd)
    def _():
        for copy in sends("odd"):
            copy.wait_send()
        for d, j in ((1, 0), (1, 1), (1, 2), (2, 0), (2, 1)):
            for copy in relays("odd", d, j):
                copy.wait_send()

    for copy in rims:
        copy.wait_send()


def finish(new, grid, out_new, out_grid, sem):
    copies = [pltpu.make_async_copy(new, out_new, sem.at[0]), pltpu.make_async_copy(grid, out_grid, sem.at[1])]
    for copy in copies:
        copy.start()
    for copy in copies:
        copy.wait()


def solution(mesh):
    rows, cols = mesh.shape["row"], mesh.shape["col"]

    def shards(p2_panel, density, pattern, x_basis, x_offset, x_extent, y_basis, y_offset, y_extent):
        outside = pl.BlockSpec(memory_space=pltpu.HBM)
        inside = pl.BlockSpec(memory_space=pltpu.VMEM)
        new, grid = pl.pallas_call(
            functools.partial(kernel, rows, cols),
            out_shape=(pltpu.VMEM((WC * BS, PANEL), BF16), pltpu.VMEM((SX, TILE), F32)),
            in_specs=[outside] * 9,
            out_specs=(inside, inside),
            scratch_shapes=[
                pltpu.VMEM((PANEL, W * BS), BF16),
                pltpu.VMEM((WC * BS, PANEL), BF16),
                pltpu.VMEM((BR, W), jnp.int32),
                pltpu.VMEM((32, PANEL), BF16),
                pltpu.VMEM((32, WC * BS), BF16),
                pltpu.SMEM((BR,), jnp.int32),
                pltpu.SMEM((BR,), jnp.int32),
                pltpu.SMEM((1, WC), jnp.int32),
                pltpu.SMEM((1, WC), jnp.int32),
                pltpu.VMEM((WC * BS, PANEL), BF16),
                pltpu.VMEM((IN_ROWS, PANEL), BF16),
                pltpu.VMEM((IN_ROWS, PANEL), BF16),
                pltpu.VMEM((WC * BS, PANEL), F32),
                pltpu.VMEM((CELLS, PANEL), BF16),
                pltpu.VMEM((2 * TILE, WC * BS), BF16),
                pltpu.VMEM((BR, PANEL), F32),
                pltpu.VMEM((CELLS, 2 * TILE), F32),
                pltpu.VMEM((2, MARGIN, TILE), F32),
                pltpu.VMEM((4, MARGIN, TILE), F32),
                pltpu.VMEM((4, MARGIN // 4, TILE), F32),
                pltpu.VMEM((4, MARGIN // 4, TILE), F32),
                pltpu.VMEM((2 * TILE, PANEL), F32),
                pltpu.VMEM((2 * TILE, PANEL), BF16),
                pltpu.SemaphoreType.DMA((15,)),
                pltpu.SemaphoreType.DMA((16,)),
                pltpu.SemaphoreType.DMA((8,)),
                pltpu.SemaphoreType.DMA((8,)),
                pltpu.SemaphoreType.DMA((8,)),
                pltpu.SemaphoreType.DMA((8,)),
                pltpu.SemaphoreType.REGULAR((6,)),
            ],
            compiler_params=pltpu.CompilerParams(
                collective_id=0, has_side_effects=True, vmem_limit_bytes=62914560
            ),
        )(
            p2_panel, density.T, pattern, x_basis.T, x_offset, x_extent, y_basis[0].T, y_offset, y_extent
        )
        new, grid = pl.pallas_call(
            finish,
            out_shape=(
                jax.ShapeDtypeStruct((WC * BS, PANEL), BF16),
                jax.ShapeDtypeStruct((SX, TILE), F32),
            ),
            in_specs=[inside, inside],
            out_specs=(outside, outside),
            scratch_shapes=[pltpu.SemaphoreType.DMA((2,))],
            compiler_params=pltpu.CompilerParams(vmem_limit_bytes=4 * 1024 * 1024),
        )(new, grid)
        return new.T, grid

    placed = (
        P("row", None),
        P("row", "col"),
        P("row", None),
        P("row", None),
        P("row"),
        P("row"),
        P("row", "col", None),
        P("row", "col"),
        P("row", "col"),
    )
    return jax.shard_map(
        shards,
        mesh=mesh,
        in_specs=placed,
        out_specs=(P("row", "col"), P("row", "col")),
        check_vma=False,
    )
```

```python
import functools

import jax
import jax.numpy as jnp
from jax import lax
from jax.experimental import pallas as pl
from jax.experimental.pallas import tpu as pltpu
from jax.sharding import PartitionSpec as P

MESH = pl.DeviceIdType.MESH
BS = 64
BR = 8
CLASSES = 8
WC = 7
W = 56
PANEL = 512
TILE = 128
CELLS = 192
SX = 128
MARGIN = 32
F32 = jnp.float32
BF16 = jnp.bfloat16

UP = {
    1: ((320, 128), (192, 128), (64, 128)),
    2: ((320, 128), (192, 128), (128, 64)),
    3: ((320, 128), (192, 128)),
}
DOWN = {
    1: ((0, 128), (128, 128), (256, 128)),
    2: ((0, 128), (128, 128), (256, 64)),
    3: ((0, 128), (128, 128)),
}
FIRST = {1: 0, 2: 3, 3: 6}
BASE = {1: 0, 2: 384, 3: 704}
IN_ROWS = 960


def dot_nt(left, right):
    return lax.dot_general(left, right, (((1,), (1,)), ((), ())), preferred_element_type=F32)


def kernel(
    rows, cols,
    p2, dens, pat, xb, xo, xe, yb, yo, ye,
    out_new, out_grid,
    s, dv, pv, xbv, ybv, xov, xev, yov, yev,
    own, up_in, down_in, acc, spread_x, spread_y, mask_rows, ext, packed, halo, corner_out, corner_in, half_part, half,
    load_sem, send_sem, up_sem, down_sem, hsend_sem, halo_sem, ready_sem,
):
    r = lax.axis_index("row")
    c = lax.axis_index("col")
    even = lax.rem(r, 2) == 0
    odd = lax.rem(r, 2) == 1

    def at(dr, dc):
        return (lax.rem(r + (dr + rows), rows), lax.rem(c + (dc + cols), cols))

    barrier = pltpu.get_barrier_semaphore()
    along_row = [(-1, 0), (1, 0), (-2, 0), (2, 0)]
    aside = [(0, -1), (0, 1), (-1, -1), (1, 1), (-1, 1), (1, -1)]
    for dr, dc in along_row:
        pl.semaphore_signal(barrier, inc=1, device_id=at(dr, dc), device_id_type=MESH)
    before = len(along_row)
    for dr, dc in aside:
        other = at(dr, dc)
        before = before + jnp.where(other[1] < c, 1, 0)

        @pl.when(other[1] > c)
        def _():
            pl.semaphore_signal(barrier, inc=1, device_id=other, device_id_type=MESH)

    loads = []
    for number, (source, target) in enumerate(
        ((dens, dv), (pat, pv), (xb, xbv), (yb, ybv), (xo, xov), (xe, xev), (yo, yov), (ye, yev))
    ):
        loads.append(pltpu.make_async_copy(source, target, load_sem.at[number]))
    square_loads = {}
    for number, block in enumerate((3, 2, 4, 1, 5, 0, 6)):
        part = pl.ds(block * PANEL, PANEL)
        square_loads[block] = pltpu.make_async_copy(p2.at[:, part], s.at[:, part], load_sem.at[8 + number])
    for load in loads:
        load.start()
    for block in (3, 2, 4, 1, 5, 0, 6):
        square_loads[block].start()

    loads[1].wait()
    pattern = pv[...].astype(F32).astype(BF16)
    position = lax.broadcasted_iota(jnp.int32, (BR, W), 1)
    slot = lax.broadcasted_iota(jnp.int32, (BR, W), 0)
    chosen = jnp.where(position == slot * CLASSES + c, 1.0, 0.0).astype(BF16)
    by_slot = dot_nt(chosen, pattern)
    block_row = lax.broadcasted_iota(jnp.int32, (BR, PANEL), 0)
    row_block = lax.broadcasted_iota(jnp.int32, (BR, PANEL), 1) // BS
    widen = jnp.where(block_row == row_block, 1.0, 0.0).astype(BF16)
    mask_rows[...] = jnp.dot(by_slot.astype(BF16), widen, preferred_element_type=F32)

    loads[0].wait()
    for k in range(WC):
        part = pl.ds(k * BS, BS)
        keep = jnp.broadcast_to(mask_rows[k : k + 1, :], (BS, PANEL)).astype(BF16)
        own[part, :] = dv[part, :] * keep

    pl.semaphore_wait(barrier, before)

    def send(source, landing, sem, number, place):
        return pltpu.make_async_remote_copy(
            src_ref=source,
            dst_ref=landing,
            send_sem=send_sem.at[number],
            recv_sem=sem,
            device_id=place,
            device_id_type=MESH,
        )

    sides = {
        "even": (UP, up_in, up_sem, 1),
        "odd": (DOWN, down_in, down_sem, -1),
    }

    def landing(kind, d, chunk):
        first, count = chunk
        start = BASE[d] + first - (d * BS if kind == "even" else 0)
        return sides[kind][1].at[pl.ds(start, count)]

    def sends(kind):
        chunks, _, sem, sign = sides[kind]
        other = "odd" if kind == "even" else "even"
        other_chunks, _, other_sem, _ = sides[other]
        found = []
        for j in range(3):
            one, two = FIRST[1] + j, FIRST[2] + j
            far, near, back = chunks[2][j], chunks[1][j], other_chunks[1][j]
            found.append(send(own.at[pl.ds(*far)], landing(kind, 2, far), sem.at[two], 3 + j, at(2 * sign, 0)))
            found.append(send(own.at[pl.ds(*back)], landing(other, 1, back), other_sem.at[one], 6 + j, at(-sign, 0)))
            found.append(send(own.at[pl.ds(*near)], landing(kind, 1, near), sem.at[one], j, at(sign, 0)))
        return found

    @pl.when(even)
    def _():
        for copy in sends("even"):
            copy.start()

    @pl.when(odd)
    def _():
        for copy in sends("odd"):
            copy.start()

    for number, (dr, dc) in enumerate(aside):
        other = at(dr, dc)

        @pl.when(other[1] < c)
        def _():
            pl.semaphore_signal(ready_sem.at[number ^ 1], inc=1, device_id=other, device_id_type=MESH)

    def relays(kind, d, j):
        chunks, _, sem, sign = sides[kind]
        found = []

        def relay(to, number, place):
            chunk = chunks[to][j]
            found.append(
                send(landing(kind, d, chunk), landing(kind, to, chunk), sem.at[FIRST[to] + j], number, place)
            )

        if d == 1:
            if j < 2:
                relay(3, 9 + j, at(2 * sign, 0))
            relay(2, 11 + j, at(sign, 0))
        if d == 2 and j < 2:
            relay(3, 14 + j, at(sign, 0))
        return found

    def arrived(mine, kind, d, j):
        chunks, _, sem, _ = sides[kind]
        place = landing(kind, d, chunks[d][j])
        send(place, place, sem.at[FIRST[d] + j], 0, at(-1, 0)).wait_recv()
        if d < 3 and kind == mine:
            for copy in relays(kind, d, j):
                copy.start()

    position = lax.broadcasted_iota(jnp.int32, (W, PANEL), 0)
    natural = lax.broadcasted_iota(jnp.int32, (W, PANEL), 1) // BS
    for block in (3, 2, 4, 1, 5, 0, 6):
        square_loads[block].wait()
        chosen = jnp.where(position == natural + block * BR, 1.0, 0.0).astype(BF16)
        mask = jnp.dot(pattern, chosen, preferred_element_type=F32)
        for i in range(BR):
            keep = jnp.broadcast_to(mask[i : i + 1, :], (BS, PANEL)).astype(BF16)
            part = pl.ds(i * BS, BS)
            s[part, pl.ds(block * PANEL, PANEL)] = s[part, pl.ds(block * PANEL, PANEL)] * keep

    parity = lax.rem(c, 2)
    to_row = lax.broadcasted_iota(jnp.int32, (BS, TILE), 0)
    from_lane = lax.broadcasted_iota(jnp.int32, (BS, TILE), 1)
    pick = jnp.where(from_lane == to_row + parity * BS, -1.5, 0.0).astype(BF16)
    acc[...] = dot_nt(own[...], s[:, pl.ds(3 * PANEL, PANEL)])
    for k in range(WC):
        start = pl.multiple_of(k * PANEL + (c // 2) * TILE, TILE)
        part = pl.ds(k * BS, BS)
        acc[part, :] = acc[part, :] + dot_nt(pick, s[:, pl.ds(start, TILE)])

    def gather(kind, d, parts):
        chunks = [sides[kind][0][d][j] for j in parts]
        first = min(chunk[0] for chunk in chunks)
        count = sum(chunk[1] for chunk in chunks)
        block = 3 - d if kind == "even" else 3 + d
        part = pl.ds(first - d * BS if kind == "even" else first + d * BS, count)
        place = landing(kind, d, (first, count))
        acc[part, :] = acc[part, :] + dot_nt(place[...], s[:, pl.ds(block * PANEL, PANEL)])

    for load in loads[2:]:
        load.wait()
    step_ids = lax.broadcasted_iota(jnp.int32, (2 * TILE, 32), 1)
    row_ids = lax.broadcasted_iota(jnp.int32, (2 * TILE, 32), 0)
    cell_ids = jnp.where(
        row_ids < CELLS - MARGIN, row_ids + MARGIN, jnp.where(row_ids < CELLS, row_ids - (CELLS - MARGIN), -1)
    )
    low = lax.broadcasted_iota(jnp.int32, (2 * TILE, TILE), 1) < BS

    def spread(values, offset, extent):
        hit = (cell_ids == offset + step_ids) & (step_ids < extent)
        onehot = jnp.where(hit, 1.0, 0.0).astype(BF16)
        return jnp.dot(onehot, values, preferred_element_type=F32)

    for t in range(4):
        part = pl.ds(t * TILE, TILE)
        pair = [spread(xbv[:, part], xov[2 * t + h], xev[2 * t + h]) for h in range(2)]
        spread_x[:, part] = jnp.where(low, pair[0], pair[1])[:CELLS].astype(BF16)
        if t < 3:
            pair = [spread(ybv[:, part], yov[0, 2 * t + h], yev[0, 2 * t + h]) for h in range(2)]
            spread_y[:, part] = jnp.where(low, pair[0], pair[1]).astype(BF16)
        else:
            part = pl.ds(t * TILE, BS)
            spread_y[:, part] = spread(ybv[:, part], yov[0, 6], yev[0, 6]).astype(BF16)

    def finish_rows(first, count):
        for k in range(first // BS, (first + count) // BS):
            part = pl.ds(k * BS, BS)
            keep = jnp.broadcast_to(mask_rows[k : k + 1, :] * -2.0, (BS, PANEL))
            out_new[part, :] = (acc[part, :] * keep).astype(BF16)
        part = pl.ds(first, count)
        return jnp.dot(spread_y[:, part], out_new[part, :], preferred_element_type=F32)

    def collect(mine):
        theirs = "odd" if mine == "even" else "even"
        steps = (
            (theirs, 1, (0, 1, 2)), (mine, 1, (0,)), (mine, 2, (0,)), (mine, 1, (1,)), (mine, 2, (1,)),
            (theirs, 2, (0, 1)), (theirs, 3, (0, 1)), (mine, 2, (2,)), (mine, 1, (2,)), (theirs, 2, (2,)),
            (mine, 3, (0,)), (mine, 3, (1,)),
        )
        early, late = ((128, 320), (0, 128)) if mine == "even" else ((0, 256), (256, 192))
        for number, (kind, d, parts) in enumerate(steps):
            if number == len(steps) - 1:
                half_part[...] = finish_rows(*early)
            for j in parts:
                arrived(mine, kind, d, j)
            gather(kind, d, parts)
        half[...] = (half_part[...] + finish_rows(*late)).astype(BF16)

    @pl.when(even)
    def _():
        collect("even")

    @pl.when(odd)
    def _():
        collect("odd")

    for number, (dr, dc) in enumerate(aside):
        @pl.when(at(dr, dc)[1] > c)
        def _():
            pl.semaphore_wait(ready_sem.at[number], 1)

    half_done = half[...]
    ext[SX:, :TILE] = dot_nt(spread_x[SX:, :], half_done[:TILE])
    ext[:, TILE:] = dot_nt(spread_x[...], half_done[TILE:])

    def rim(number, source, place, box, slot):
        return pltpu.make_async_remote_copy(
            src_ref=source,
            dst_ref=box.at[slot],
            send_sem=hsend_sem.at[number],
            recv_sem=halo_sem.at[number],
            device_id=place,
            device_id_type=MESH,
        )

    rims = [
        rim(0, ext.at[pl.ds(SX, MARGIN), pl.ds(0, TILE)], at(1, 0), halo, 0),
        rim(1, ext.at[pl.ds(SX + MARGIN, MARGIN), pl.ds(0, TILE)], at(-1, 0), halo, 1),
    ]
    for copy in rims:
        copy.start()

    def pack(first_row, height, side):
        group = lax.broadcasted_iota(jnp.int32, (height, TILE), 1) // MARGIN
        joined = jnp.zeros((height, TILE), F32)
        for g in range(4):
            start = first_row + g * height
            piece = ext[start : start + height, TILE : 2 * TILE]
            turn = (MARGIN * (g - side)) % TILE
            joined = jnp.where(group == g, pltpu.roll(piece, turn, 1) if turn else piece, joined)
        return joined

    def unpack(value, g, side):
        turn = (MARGIN * (3 - g)) % TILE if side else (-MARGIN * g) % TILE
        value = pltpu.roll(value, turn, 1) if turn else value
        group = lax.broadcasted_iota(jnp.int32, value.shape, 1) // MARGIN
        return jnp.where(group == (3 if side else 0), value, 0.0)

    for number, (dr, dc) in enumerate(((1, 1), (1, -1), (-1, 1), (-1, -1))):
        corner_out[number] = pack(SX if dr > 0 else SX + MARGIN, MARGIN // 4, 0 if dc > 0 else 1)
        rims.append(rim(4 + number, corner_out.at[number], at(dr, dc), corner_in, number))
        rims[-1].start()
    for number, dc in enumerate((1, -1)):
        packed[number] = pack(0, MARGIN, number)
        rims.append(rim(2 + number, packed.at[number], at(0, dc), halo, 2 + number))
        rims[-1].start()
    ext[:SX, :TILE] = dot_nt(spread_x[:SX, :], half_done[:TILE])

    for number in range(4):
        rim(number, halo.at[number], at(1, 0), halo, number).wait_recv()
    for g in range(4):
        value = ext[g * MARGIN : (g + 1) * MARGIN, :TILE]
        value = value + unpack(halo[2], g, 0) + unpack(halo[3], g, 1)
        if g in (0, 3):
            value = value + halo[0 if g == 0 else 1]
        out_grid[g * MARGIN : (g + 1) * MARGIN, :] = value
    for number in range(4):
        rim(4 + number, corner_in.at[number], at(1, 0), corner_in, number).wait_recv()
    height = MARGIN // 4
    for start, pair in ((0, (0, 1)), (SX - MARGIN, (2, 3))):
        for g in range(4):
            part = pl.ds(start + g * height, height)
            rest = unpack(corner_in[pair[0]], g, 0) + unpack(corner_in[pair[1]], g, 1)
            out_grid[part, :] = out_grid[part, :] + rest

    @pl.when(even)
    def _():
        for copy in sends("even"):
            copy.wait_send()
        for d, j in ((1, 0), (1, 1), (1, 2), (2, 0), (2, 1)):
            for copy in relays("even", d, j):
                copy.wait_send()

    @pl.when(odd)
    def _():
        for copy in sends("odd"):
            copy.wait_send()
        for d, j in ((1, 0), (1, 1), (1, 2), (2, 0), (2, 1)):
            for copy in relays("odd", d, j):
                copy.wait_send()

    for copy in rims:
        copy.wait_send()


def finish(new, grid, out_new, out_grid, sem):
    copies = [pltpu.make_async_copy(new, out_new, sem.at[0]), pltpu.make_async_copy(grid, out_grid, sem.at[1])]
    for copy in copies:
        copy.start()
    for copy in copies:
        copy.wait()


def solution(mesh):
    rows, cols = mesh.shape["row"], mesh.shape["col"]

    def shards(p2_panel, density, pattern, x_basis, x_offset, x_extent, y_basis, y_offset, y_extent):
        outside = pl.BlockSpec(memory_space=pltpu.HBM)
        inside = pl.BlockSpec(memory_space=pltpu.VMEM)
        new, grid = pl.pallas_call(
            functools.partial(kernel, rows, cols),
            out_shape=(pltpu.VMEM((WC * BS, PANEL), BF16), pltpu.VMEM((SX, TILE), F32)),
            in_specs=[outside] * 9,
            out_specs=(inside, inside),
            scratch_shapes=[
                pltpu.VMEM((PANEL, W * BS), BF16),
                pltpu.VMEM((WC * BS, PANEL), BF16),
                pltpu.VMEM((BR, W), jnp.int32),
                pltpu.VMEM((32, PANEL), BF16),
                pltpu.VMEM((32, WC * BS), BF16),
                pltpu.SMEM((BR,), jnp.int32),
                pltpu.SMEM((BR,), jnp.int32),
                pltpu.SMEM((1, WC), jnp.int32),
                pltpu.SMEM((1, WC), jnp.int32),
                pltpu.VMEM((WC * BS, PANEL), BF16),
                pltpu.VMEM((IN_ROWS, PANEL), BF16),
                pltpu.VMEM((IN_ROWS, PANEL), BF16),
                pltpu.VMEM((WC * BS, PANEL), F32),
                pltpu.VMEM((CELLS, PANEL), BF16),
                pltpu.VMEM((2 * TILE, WC * BS), BF16),
                pltpu.VMEM((BR, PANEL), F32),
                pltpu.VMEM((CELLS, 2 * TILE), F32),
                pltpu.VMEM((2, MARGIN, TILE), F32),
                pltpu.VMEM((4, MARGIN, TILE), F32),
                pltpu.VMEM((4, MARGIN // 4, TILE), F32),
                pltpu.VMEM((4, MARGIN // 4, TILE), F32),
                pltpu.VMEM((2 * TILE, PANEL), F32),
                pltpu.VMEM((2 * TILE, PANEL), BF16),
                pltpu.SemaphoreType.DMA((15,)),
                pltpu.SemaphoreType.DMA((16,)),
                pltpu.SemaphoreType.DMA((8,)),
                pltpu.SemaphoreType.DMA((8,)),
                pltpu.SemaphoreType.DMA((8,)),
                pltpu.SemaphoreType.DMA((8,)),
                pltpu.SemaphoreType.REGULAR((6,)),
            ],
            compiler_params=pltpu.CompilerParams(
                collective_id=0, has_side_effects=True, vmem_limit_bytes=62914560
            ),
        )(
            p2_panel, density.T, pattern, x_basis.T, x_offset, x_extent, y_basis[0].T, y_offset, y_extent
        )
        new, grid = pl.pallas_call(
            finish,
            out_shape=(
                jax.ShapeDtypeStruct((WC * BS, PANEL), BF16),
                jax.ShapeDtypeStruct((SX, TILE), F32),
            ),
            in_specs=[inside, inside],
            out_specs=(outside, outside),
            scratch_shapes=[pltpu.SemaphoreType.DMA((2,))],
            compiler_params=pltpu.CompilerParams(vmem_limit_bytes=4 * 1024 * 1024),
        )(new, grid)
        return new.T, grid

    placed = (
        P("row", None),
        P("row", "col"),
        P("row", None),
        P("row", None),
        P("row"),
        P("row"),
        P("row", "col", None),
        P("row", "col"),
        P("row", "col"),
    )
    return jax.shard_map(
        shards,
        mesh=mesh,
        in_specs=placed,
        out_specs=(P("row", "col"), P("row", "col")),
        check_vma=False,
    )
```

```python
import functools

import jax
import jax.numpy as jnp
from jax import lax
from jax.experimental import pallas as pl
from jax.experimental.pallas import tpu as pltpu
from jax.sharding import PartitionSpec as P

MESH = pl.DeviceIdType.MESH
BS = 64
BR = 8
CLASSES = 8
WC = 7
W = 56
PANEL = 512
TILE = 128
CELLS = 192
SX = 128
MARGIN = 32
F32 = jnp.float32
BF16 = jnp.bfloat16

UP = {
    1: ((320, 128), (192, 128), (64, 128)),
    2: ((320, 128), (192, 128), (128, 64)),
    3: ((320, 128), (192, 128)),
}
DOWN = {
    1: ((0, 128), (128, 128), (256, 128)),
    2: ((0, 128), (128, 128), (256, 64)),
    3: ((0, 128), (128, 128)),
}
FIRST = {1: 0, 2: 3, 3: 6}
BASE = {1: 0, 2: 384, 3: 704}
IN_ROWS = 960


def dot_nt(left, right):
    return lax.dot_general(left, right, (((1,), (1,)), ((), ())), preferred_element_type=F32)


def kernel(
    rows, cols,
    p2, dens, pat, xb, xo, xe, yb, yo, ye,
    out_new, out_grid,
    s, dv, pv, xbv, ybv, xov, xev, yov, yev,
    own, up_in, down_in, acc, spread_x, spread_y, mask_rows, ext, packed, halo, corner_out, corner_in, half_part, half,
    load_sem, send_sem, up_sem, down_sem, hsend_sem, halo_sem, ready_sem,
):
    r = lax.axis_index("row")
    c = lax.axis_index("col")
    even = lax.rem(r, 2) == 0
    odd = lax.rem(r, 2) == 1

    def at(dr, dc):
        return (lax.rem(r + (dr + rows), rows), lax.rem(c + (dc + cols), cols))

    barrier = pltpu.get_barrier_semaphore()
    along_row = [(-1, 0), (1, 0), (-2, 0), (2, 0)]
    aside = [(0, -1), (0, 1), (-1, -1), (1, 1), (-1, 1), (1, -1)]
    for dr, dc in along_row:
        pl.semaphore_signal(barrier, inc=1, device_id=at(dr, dc), device_id_type=MESH)
    before = len(along_row)
    for dr, dc in aside:
        other = at(dr, dc)
        before = before + jnp.where(other[1] < c, 1, 0)

        @pl.when(other[1] > c)
        def _():
            pl.semaphore_signal(barrier, inc=1, device_id=other, device_id_type=MESH)

    loads = []
    for number, (source, target) in enumerate(
        ((dens, dv), (pat, pv), (xb, xbv), (yb, ybv), (xo, xov), (xe, xev), (yo, yov), (ye, yev))
    ):
        loads.append(pltpu.make_async_copy(source, target, load_sem.at[number]))
    square_loads = {}
    for number, block in enumerate((3, 2, 4, 1, 5, 0, 6)):
        part = pl.ds(block * PANEL, PANEL)
        square_loads[block] = pltpu.make_async_copy(p2.at[:, part], s.at[:, part], load_sem.at[8 + number])
    for load in loads:
        load.start()
    for block in (3, 2, 4, 1, 5, 0, 6):
        square_loads[block].start()

    loads[1].wait()
    pattern = pv[...].astype(F32).astype(BF16)
    position = lax.broadcasted_iota(jnp.int32, (BR, W), 1)
    slot = lax.broadcasted_iota(jnp.int32, (BR, W), 0)
    chosen = jnp.where(position == slot * CLASSES + c, 1.0, 0.0).astype(BF16)
    by_slot = dot_nt(chosen, pattern)
    block_row = lax.broadcasted_iota(jnp.int32, (BR, PANEL), 0)
    row_block = lax.broadcasted_iota(jnp.int32, (BR, PANEL), 1) // BS
    widen = jnp.where(block_row == row_block, 1.0, 0.0).astype(BF16)
    mask_rows[...] = jnp.dot(by_slot.astype(BF16), widen, preferred_element_type=F32)

    loads[0].wait()
    for k in range(WC):
        part = pl.ds(k * BS, BS)
        keep = jnp.broadcast_to(mask_rows[k : k + 1, :], (BS, PANEL)).astype(BF16)
        own[part, :] = dv[part, :] * keep

    pl.semaphore_wait(barrier, before)

    def send(source, landing, sem, number, place):
        return pltpu.make_async_remote_copy(
            src_ref=source,
            dst_ref=landing,
            send_sem=send_sem.at[number],
            recv_sem=sem,
            device_id=place,
            device_id_type=MESH,
        )

    sides = {
        "even": (UP, up_in, up_sem, 1),
        "odd": (DOWN, down_in, down_sem, -1),
    }

    def landing(kind, d, chunk):
        first, count = chunk
        start = BASE[d] + first - (d * BS if kind == "even" else 0)
        return sides[kind][1].at[pl.ds(start, count)]

    def sends(kind):
        chunks, _, sem, sign = sides[kind]
        other = "odd" if kind == "even" else "even"
        other_chunks, _, other_sem, _ = sides[other]
        found = []
        for j in range(3):
            one, two = FIRST[1] + j, FIRST[2] + j
            far, near, back = chunks[2][j], chunks[1][j], other_chunks[1][j]
            found.append(send(own.at[pl.ds(*far)], landing(kind, 2, far), sem.at[two], 3 + j, at(2 * sign, 0)))
            found.append(send(own.at[pl.ds(*back)], landing(other, 1, back), other_sem.at[one], 6 + j, at(-sign, 0)))
            found.append(send(own.at[pl.ds(*near)], landing(kind, 1, near), sem.at[one], j, at(sign, 0)))
        return found

    @pl.when(even)
    def _():
        for copy in sends("even"):
            copy.start()

    @pl.when(odd)
    def _():
        for copy in sends("odd"):
            copy.start()

    for number, (dr, dc) in enumerate(aside):
        other = at(dr, dc)

        @pl.when(other[1] < c)
        def _():
            pl.semaphore_signal(ready_sem.at[number ^ 1], inc=1, device_id=other, device_id_type=MESH)

    def relays(kind, d, j):
        chunks, _, sem, sign = sides[kind]
        found = []

        def relay(to, number, place):
            chunk = chunks[to][j]
            found.append(
                send(landing(kind, d, chunk), landing(kind, to, chunk), sem.at[FIRST[to] + j], number, place)
            )

        if d == 1:
            if j < 2:
                relay(3, 9 + j, at(2 * sign, 0))
            relay(2, 11 + j, at(sign, 0))
        if d == 2 and j < 2:
            relay(3, 14 + j, at(sign, 0))
        return found

    def arrived(mine, kind, d, j):
        chunks, _, sem, _ = sides[kind]
        place = landing(kind, d, chunks[d][j])
        send(place, place, sem.at[FIRST[d] + j], 0, at(-1, 0)).wait_recv()
        if d < 3 and kind == mine:
            for copy in relays(kind, d, j):
                copy.start()

    position = lax.broadcasted_iota(jnp.int32, (W, PANEL), 0)
    natural = lax.broadcasted_iota(jnp.int32, (W, PANEL), 1) // BS
    for block in (3, 2, 4, 1, 5, 0, 6):
        square_loads[block].wait()
        chosen = jnp.where(position == natural + block * BR, 1.0, 0.0).astype(BF16)
        mask = jnp.dot(pattern, chosen, preferred_element_type=F32)
        for i in range(BR):
            keep = jnp.broadcast_to(mask[i : i + 1, :], (BS, PANEL)).astype(BF16)
            part = pl.ds(i * BS, BS)
            s[part, pl.ds(block * PANEL, PANEL)] = s[part, pl.ds(block * PANEL, PANEL)] * keep

    parity = lax.rem(c, 2)
    to_row = lax.broadcasted_iota(jnp.int32, (BS, TILE), 0)
    from_lane = lax.broadcasted_iota(jnp.int32, (BS, TILE), 1)
    pick = jnp.where(from_lane == to_row + parity * BS, -1.5, 0.0).astype(BF16)
    acc[...] = dot_nt(own[...], s[:, pl.ds(3 * PANEL, PANEL)])
    for k in range(WC):
        start = pl.multiple_of(k * PANEL + (c // 2) * TILE, TILE)
        part = pl.ds(k * BS, BS)
        acc[part, :] = acc[part, :] + dot_nt(pick, s[:, pl.ds(start, TILE)])

    def gather(kind, d, parts):
        chunks = [sides[kind][0][d][j] for j in parts]
        first = min(chunk[0] for chunk in chunks)
        count = sum(chunk[1] for chunk in chunks)
        block = 3 - d if kind == "even" else 3 + d
        part = pl.ds(first - d * BS if kind == "even" else first + d * BS, count)
        place = landing(kind, d, (first, count))
        acc[part, :] = acc[part, :] + dot_nt(place[...], s[:, pl.ds(block * PANEL, PANEL)])

    for load in loads[2:]:
        load.wait()
    step_ids = lax.broadcasted_iota(jnp.int32, (2 * TILE, 32), 1)
    row_ids = lax.broadcasted_iota(jnp.int32, (2 * TILE, 32), 0)
    cell_ids = jnp.where(
        row_ids < CELLS - MARGIN, row_ids + MARGIN, jnp.where(row_ids < CELLS, row_ids - (CELLS - MARGIN), -1)
    )
    low = lax.broadcasted_iota(jnp.int32, (2 * TILE, TILE), 1) < BS

    def spread(values, offset, extent):
        hit = (cell_ids == offset + step_ids) & (step_ids < extent)
        onehot = jnp.where(hit, 1.0, 0.0).astype(BF16)
        return jnp.dot(onehot, values, preferred_element_type=F32)

    for t in range(4):
        part = pl.ds(t * TILE, TILE)
        pair = [spread(xbv[:, part], xov[2 * t + h], xev[2 * t + h]) for h in range(2)]
        spread_x[:, part] = jnp.where(low, pair[0], pair[1])[:CELLS].astype(BF16)
        if t < 3:
            pair = [spread(ybv[:, part], yov[0, 2 * t + h], yev[0, 2 * t + h]) for h in range(2)]
            spread_y[:, part] = jnp.where(low, pair[0], pair[1]).astype(BF16)
        else:
            part = pl.ds(t * TILE, BS)
            spread_y[:, part] = spread(ybv[:, part], yov[0, 6], yev[0, 6]).astype(BF16)

    def finish_rows(first, count):
        for k in range(first // BS, (first + count) // BS):
            part = pl.ds(k * BS, BS)
            keep = jnp.broadcast_to(mask_rows[k : k + 1, :] * -2.0, (BS, PANEL))
            out_new[part, :] = (acc[part, :] * keep).astype(BF16)
        part = pl.ds(first, count)
        return jnp.dot(spread_y[:, part], out_new[part, :], preferred_element_type=F32)

    def collect(mine):
        theirs = "odd" if mine == "even" else "even"
        steps = (
            (theirs, 1, (0, 1, 2)), (mine, 1, (0,)), (mine, 2, (0,)), (mine, 1, (1,)), (mine, 2, (1,)),
            (theirs, 2, (0, 1)), (theirs, 3, (0, 1)), (mine, 2, (2,)), (mine, 1, (2,)), (theirs, 2, (2,)),
            (mine, 3, (0,)), (mine, 3, (1,)),
        )
        early, late = ((128, 320), (0, 128)) if mine == "even" else ((0, 256), (256, 192))
        for number, (kind, d, parts) in enumerate(steps):
            if number == len(steps) - 1:
                half_part[...] = finish_rows(*early)
            for j in parts:
                arrived(mine, kind, d, j)
            gather(kind, d, parts)
        half[...] = (half_part[...] + finish_rows(*late)).astype(BF16)

    @pl.when(even)
    def _():
        collect("even")

    @pl.when(odd)
    def _():
        collect("odd")

    for number, (dr, dc) in enumerate(aside):
        @pl.when(at(dr, dc)[1] > c)
        def _():
            pl.semaphore_wait(ready_sem.at[number], 1)

    half_done = half[...]
    ext[SX:, :TILE] = dot_nt(spread_x[SX:, :], half_done[:TILE])
    ext[:, TILE:] = dot_nt(spread_x[...], half_done[TILE:])

    def rim(number, source, place, box, slot):
        return pltpu.make_async_remote_copy(
            src_ref=source,
            dst_ref=box.at[slot],
            send_sem=hsend_sem.at[number],
            recv_sem=halo_sem.at[number],
            device_id=place,
            device_id_type=MESH,
        )

    for number in range(2):
        start = SX + number * MARGIN
        packed[number] = ext[start : start + MARGIN, :TILE].astype(BF16)
    rims = [rim(0, packed.at[0], at(1, 0), halo, 0), rim(1, packed.at[1], at(-1, 0), halo, 1)]
    for copy in rims:
        copy.start()

    def pack(first_row, height, side):
        group = lax.broadcasted_iota(jnp.int32, (height, TILE), 1) // MARGIN
        joined = jnp.zeros((height, TILE), F32)
        for g in range(4):
            start = first_row + g * height
            piece = ext[start : start + height, TILE : 2 * TILE]
            turn = (MARGIN * (g - side)) % TILE
            joined = jnp.where(group == g, pltpu.roll(piece, turn, 1) if turn else piece, joined)
        return joined

    def unpack(value, g, side):
        turn = (MARGIN * (3 - g)) % TILE if side else (-MARGIN * g) % TILE
        value = pltpu.roll(value, turn, 1) if turn else value
        group = lax.broadcasted_iota(jnp.int32, value.shape, 1) // MARGIN
        return jnp.where(group == (3 if side else 0), value, 0.0)

    for number, (dr, dc) in enumerate(((1, 1), (1, -1), (-1, 1), (-1, -1))):
        corner_out[number] = pack(SX if dr > 0 else SX + MARGIN, MARGIN // 4, 0 if dc > 0 else 1)
        rims.append(rim(4 + number, corner_out.at[number], at(dr, dc), corner_in, number))
        rims[-1].start()
    for number, dc in enumerate((1, -1)):
        packed[2 + number] = pack(0, MARGIN, number).astype(BF16)
        rims.append(rim(2 + number, packed.at[2 + number], at(0, dc), halo, 2 + number))
        rims[-1].start()
    ext[:SX, :TILE] = dot_nt(spread_x[:SX, :], half_done[:TILE])

    for number in range(4):
        rim(number, halo.at[number], at(1, 0), halo, number).wait_recv()
    aside_low, aside_high = halo[2].astype(F32), halo[3].astype(F32)
    for g in range(4):
        value = ext[g * MARGIN : (g + 1) * MARGIN, :TILE]
        value = value + unpack(aside_low, g, 0) + unpack(aside_high, g, 1)
        if g in (0, 3):
            value = value + halo[0 if g == 0 else 1].astype(F32)
        out_grid[g * MARGIN : (g + 1) * MARGIN, :] = value
    for number in range(4):
        rim(4 + number, corner_in.at[number], at(1, 0), corner_in, number).wait_recv()
    height = MARGIN // 4
    for start, pair in ((0, (0, 1)), (SX - MARGIN, (2, 3))):
        for g in range(4):
            part = pl.ds(start + g * height, height)
            rest = unpack(corner_in[pair[0]], g, 0) + unpack(corner_in[pair[1]], g, 1)
            out_grid[part, :] = out_grid[part, :] + rest

    @pl.when(even)
    def _():
        for copy in sends("even"):
            copy.wait_send()
        for d, j in ((1, 0), (1, 1), (1, 2), (2, 0), (2, 1)):
            for copy in relays("even", d, j):
                copy.wait_send()

    @pl.when(odd)
    def _():
        for copy in sends("odd"):
            copy.wait_send()
        for d, j in ((1, 0), (1, 1), (1, 2), (2, 0), (2, 1)):
            for copy in relays("odd", d, j):
                copy.wait_send()

    for copy in rims:
        copy.wait_send()


def finish(new, grid, out_new, out_grid, sem):
    copies = [pltpu.make_async_copy(new, out_new, sem.at[0]), pltpu.make_async_copy(grid, out_grid, sem.at[1])]
    for copy in copies:
        copy.start()
    for copy in copies:
        copy.wait()


def solution(mesh):
    rows, cols = mesh.shape["row"], mesh.shape["col"]

    def shards(p2_panel, density, pattern, x_basis, x_offset, x_extent, y_basis, y_offset, y_extent):
        outside = pl.BlockSpec(memory_space=pltpu.HBM)
        inside = pl.BlockSpec(memory_space=pltpu.VMEM)
        new, grid = pl.pallas_call(
            functools.partial(kernel, rows, cols),
            out_shape=(pltpu.VMEM((WC * BS, PANEL), BF16), pltpu.VMEM((SX, TILE), F32)),
            in_specs=[outside] * 9,
            out_specs=(inside, inside),
            scratch_shapes=[
                pltpu.VMEM((PANEL, W * BS), BF16),
                pltpu.VMEM((WC * BS, PANEL), BF16),
                pltpu.VMEM((BR, W), jnp.int32),
                pltpu.VMEM((32, PANEL), BF16),
                pltpu.VMEM((32, WC * BS), BF16),
                pltpu.SMEM((BR,), jnp.int32),
                pltpu.SMEM((BR,), jnp.int32),
                pltpu.SMEM((1, WC), jnp.int32),
                pltpu.SMEM((1, WC), jnp.int32),
                pltpu.VMEM((WC * BS, PANEL), BF16),
                pltpu.VMEM((IN_ROWS, PANEL), BF16),
                pltpu.VMEM((IN_ROWS, PANEL), BF16),
                pltpu.VMEM((WC * BS, PANEL), F32),
                pltpu.VMEM((CELLS, PANEL), BF16),
                pltpu.VMEM((2 * TILE, WC * BS), BF16),
                pltpu.VMEM((BR, PANEL), F32),
                pltpu.VMEM((CELLS, 2 * TILE), F32),
                pltpu.VMEM((4, MARGIN, TILE), BF16),
                pltpu.VMEM((4, MARGIN, TILE), BF16),
                pltpu.VMEM((4, MARGIN // 4, TILE), F32),
                pltpu.VMEM((4, MARGIN // 4, TILE), F32),
                pltpu.VMEM((2 * TILE, PANEL), F32),
                pltpu.VMEM((2 * TILE, PANEL), BF16),
                pltpu.SemaphoreType.DMA((15,)),
                pltpu.SemaphoreType.DMA((16,)),
                pltpu.SemaphoreType.DMA((8,)),
                pltpu.SemaphoreType.DMA((8,)),
                pltpu.SemaphoreType.DMA((8,)),
                pltpu.SemaphoreType.DMA((8,)),
                pltpu.SemaphoreType.REGULAR((6,)),
            ],
            compiler_params=pltpu.CompilerParams(
                collective_id=0, has_side_effects=True, vmem_limit_bytes=62914560
            ),
        )(
            p2_panel, density.T, pattern, x_basis.T, x_offset, x_extent, y_basis[0].T, y_offset, y_extent
        )
        new, grid = pl.pallas_call(
            finish,
            out_shape=(
                jax.ShapeDtypeStruct((WC * BS, PANEL), BF16),
                jax.ShapeDtypeStruct((SX, TILE), F32),
            ),
            in_specs=[inside, inside],
            out_specs=(outside, outside),
            scratch_shapes=[pltpu.SemaphoreType.DMA((2,))],
            compiler_params=pltpu.CompilerParams(vmem_limit_bytes=4 * 1024 * 1024),
        )(new, grid)
        return new.T, grid

    placed = (
        P("row", None),
        P("row", "col"),
        P("row", None),
        P("row", None),
        P("row"),
        P("row"),
        P("row", "col", None),
        P("row", "col"),
        P("row", "col"),
    )
    return jax.shard_map(
        shards,
        mesh=mesh,
        in_specs=placed,
        out_specs=(P("row", "col"), P("row", "col")),
        check_vma=False,
    )
```
